32 devices in a mesh: blk: 8 (over y, x, core), virt: 4 (over z).
Axes of the slice: x: 2, y: 2, z: 4, core: 2. Of those that a mesh axis runs over, the one named last changes fastest.
Arguments:
- integral_tiles: bfloat16 [4, 1024, 128, 128], P('virt', 'blk'), may hold values from -0.1875 to 0.1875
- tile_panel: int32 [4, 1024, 1], P('virt', 'blk'), may hold values from 0 to 7; in each aligned block of 128 rows (0 to 127, 128 to 255, ..., all dimensions but the last counted through in order) at most 32 rows name the same one
- tile_row: int32 [4, 1024], P('virt', 'blk'), may hold values from 0 to 11
- tile_col: int32 [4, 1024], P('virt', 'blk'), may hold values from 0 to 7
- green_factor: float32 [1024, 8192], P('blk'), may hold values from -6 to 6
- window_start: int32 [1], replicated, may hold values from 0 to 7168
Outputs:
- response: float32 [12288, 1536], P(('blk', 'virt'))
The draws below stay inside these ranges and needn't reach their ends.
Inputs may be any that keep to these rules, and one draw needn't show every extreme that they name: `tile_panel`: within the tiles of one device, at most 32 name the same panel, and some device has exactly 32 for one panel.
All inputs are finite; a program needn't handle non-finite values.
Results may differ from the reference program's by a relative error of at most 0.0019.
Values may be sent and summed in bfloat16 or wider, within the bound.
No kernel may reach another device: no remote copies, remote signals or barrier semaphores. Data moves between devices by JAX's collectives and lax.ppermute only.
A program may use at most 128 MiB of HBM per device.

```python
import math
import jax
import jax.numpy as jnp
import numpy as np
from jax import lax

TILE = 128
NOCC = 1024
NALL = 8192
STOPS = 8
PANEL = 1536
TILE_DEV = 128
CAP = 32
NTILES = 1024
NBASIS = 1024
N_BLK = 8
N_VIRT = 4


def place_ends(values, stream_key, least, high):
    longest = values.shape.index(max(values.shape))
    spots = []
    for shift in (0, 1):
        where = [jax.random.randint(jax.random.fold_in(stream_key, axis), (), 0, length) for axis, length in enumerate(values.shape)]
        where[longest] = (where[longest] + shift) % values.shape[longest]
        spots.append(tuple(where))
    return values.at[spots[0]].set(least).at[spots[1]].set(high)


def block_levels(rng, shape, pieces, least, top_value):
    def one(position, parts):
        steps = jax.random.uniform(jax.random.fold_in(jax.random.fold_in(rng, 6), position), (parts,), jnp.float32, least / len(pieces), top_value / len(pieces))
        return jnp.repeat(jnp.exp(steps), shape[position] // parts).reshape((-1,) + (1,) * (len(shape) - position - 1))

    factor_of = one(*pieces[0])
    for cut in pieces[1:]:
        factor_of = factor_of * one(*cut)
    return factor_of


def assign_block(own_key, own, number, rows, count, top, bound, lean):
    sequence = jax.random.permutation(own_key, count)
    crowded, common = portions_of(count, rows * top, bound, lean, True), portions_of(count, rows * top, bound, lean, False)
    places = jnp.arange(count)

    def named(lengths, turn):
        used = int((lengths > 0).sum())
        fixed = max(1, used // 4)
        moved = fixed + (places - fixed + turn * (used - fixed)) % max(1, count - fixed)
        return jnp.zeros((count,), jnp.int32).at[sequence[jnp.where(places < fixed, places, moved)]].set(jnp.asarray(lengths, jnp.int32))

    lengths = jnp.where(number % 4 == 0, named(crowded, number // 4), named(common, number - number // 4 - 1))
    mixed = jax.random.permutation(jax.random.fold_in(own, 3), count)
    source_of, sink = mixed[0:count // 2 * 2:2], mixed[1:count // 2 * 2:2]
    margin = jnp.minimum(lengths[source_of] - 1, bound - lengths[sink]) // 2
    margin = jnp.where((source_of == sequence[0]) | (sink == sequence[0]) | (lengths[sink] == 0), 0, jnp.maximum(margin, 0))
    moved = jax.random.randint(jax.random.fold_in(own, 4), (count // 2,), 0, 1 << 20) % (margin + 1)
    lengths = lengths.at[source_of].add(-moved).at[sink].add(moved)
    labels = jnp.searchsorted(jnp.cumsum(lengths), jnp.arange(rows * top), side="right").astype(jnp.int32)
    table = labels.reshape(top, rows).T
    table = table[jax.random.permutation(jax.random.fold_in(own, 1), rows)]
    turn = jax.random.randint(jax.random.fold_in(own, 2), (rows, 1), 0, top)
    return jnp.take_along_axis(table, (jnp.arange(top)[None, :] + turn) % top, axis=1)


def portions_of(number_of, total, limit, lean, full):
    portions = [(1 << 20) // math.isqrt(grade ** lean) + 1 for grade in range(1, number_of + 1)]
    largest = limit if full else min(limit, max(-(-total // number_of), total * portions[0] // sum(portions)))
    least = 1 if total - largest >= number_of - 1 else 0
    holding, rest = [largest] + [least] * (number_of - 1), total - largest - least * (number_of - 1)
    while rest > 0:
        movable = [i for i in range(1, number_of) if holding[i] < largest] or [i for i in range(1, number_of) if holding[i] < limit]
        mass, budget = sum([portions[i] for i in movable]), rest
        for i in movable:
            addition = min(limit - holding[i], max(1, budget * portions[i] // mass), rest)
            holding[i] = holding[i] + addition
            rest = rest - addition
    return np.array(holding)


def bell_draw(rng, dims, width, reach, cuts=(), held_as=jnp.bfloat16):
    gain = block_levels(rng, dims, cuts, -0.22, 0.18) if cuts else 1.0
    array = jax.random.normal(rng, dims, jnp.float32) * width * gain
    return jnp.minimum(jnp.maximum(array, -reach), reach).astype(held_as)


def setup_inputs(seed: int = 0) -> dict:
    key_of = jax.random.split(jax.random.key(seed), 7)
    integral_tiles = bell_draw(key_of[0], (N_VIRT, NTILES, TILE, TILE), (STOPS * TILE) ** -0.5, 0.1875, ((0, 4), (1, 8)))
    tile_panel_keys = jax.random.split(jax.random.fold_in(key_of[1], 1), N_VIRT * NTILES // TILE_DEV)
    tile_panel_turns = jax.random.permutation(jax.random.fold_in(key_of[1], 3), N_VIRT * NTILES // TILE_DEV)
    tile_panel = jax.vmap(lambda own, number: assign_block(jax.random.fold_in(key_of[1], 2), own, number, TILE_DEV, N_BLK, 1, CAP, 2))(tile_panel_keys, tile_panel_turns).reshape((N_VIRT, NTILES, 1))
    tile_row = place_ends(jax.random.randint(key_of[2], (N_VIRT, NTILES), 0, PANEL // TILE), jax.random.fold_in(key_of[2], 1), 0, (PANEL // TILE) - 1).astype(jnp.int32)
    tile_col = place_ends(jax.random.randint(key_of[3], (N_VIRT, NTILES), 0, STOPS), jax.random.fold_in(key_of[3], 1), 0, STOPS - 1).astype(jnp.int32)
    green_factor = bell_draw(key_of[4], (NBASIS, NALL), 1.0, 6.0, ((0, 8),), jnp.float32)
    window_start = jax.random.randint(key_of[5], (1,), 0, NALL - NOCC + 1).astype(jnp.int32)
    return dict(integral_tiles=integral_tiles, tile_panel=tile_panel, tile_row=tile_row, tile_col=tile_col, green_factor=green_factor, window_start=window_start)


def reference(integral_tiles, tile_panel, tile_row, tile_col, green_factor, window_start):
    blocks = PANEL // TILE
    middle = STOPS // 2
    window = lax.dynamic_slice_in_dim(green_factor, window_start[0].astype(jnp.int32), NOCC, 1)
    basis_rows = window.reshape(N_BLK, TILE, NOCC)
    virt_ids = jnp.broadcast_to(jnp.arange(N_VIRT, dtype=jnp.int32)[:, None], tile_row.shape)
    dense = jnp.zeros((N_VIRT, N_BLK, blocks, STOPS, TILE, TILE), jnp.float32)
    dense = dense.at[virt_ids, tile_panel[:, :, 0], tile_row, tile_col].add(integral_tiles.astype(jnp.float32))
    factor = -1.0 / math.sqrt(N_VIRT * NOCC)

    def one_panel(panel_at):
        nearby_ids = (panel_at + jnp.arange(STOPS, dtype=jnp.int32) - middle) % N_BLK
        nearby = basis_rows[nearby_ids]
        owned = dense[:, panel_at]
        coupled = jnp.einsum('vasij,sjn->vain', owned, nearby, precision=lax.Precision.HIGHEST)
        coupled = coupled.reshape(N_VIRT, PANEL, NOCC).astype(jnp.bfloat16).astype(jnp.float32)
        gram_block = jnp.einsum('vpn,vqn->pq', coupled, coupled)
        return gram_block * factor
    stacked = lax.map(one_panel, jnp.arange(N_BLK, dtype=jnp.int32))
    return stacked.reshape(N_BLK * PANEL, PANEL)
```

```python
import functools
import math

import jax
import jax.numpy as jnp
from jax import lax
from jax.experimental import pallas as pl
from jax.experimental.pallas import tpu as pltpu
from jax.sharding import PartitionSpec as P


NOCC = 1024
STOPS = 8
PANEL = 1536
LABEL_ROWS = 16
AXES = ("blk", "virt")


def rounds_of(slots):
    if slots < 8:
        return [(0, slots)]
    first, second = slots // 2, slots - slots // 8
    return [(0, first), (first, second), (second, slots)]


def offset_order(count):
    def key(offset):
        chip = offset // 2
        return (bin(chip).count("1") or count, offset % 2, chip)

    return sorted(range(count), key=key)


def partner(block, offset, count):
    return block ^ offset if count & (count - 1) == 0 else (block + offset) % count


def place_of(panel, slab, virt_count):
    return (2 * (panel // 2) + slab % 2) * virt_count + 2 * (slab // 2) + panel % 2


def pack_kernel(count, slots, rounds, order, panel_s, panel_row, code_row, tiles, *rest):
    made = rest[: len(rounds) * count]
    held, label_rows, label_blocks, slot_tile, used, in_sem, out_sem, label_sem = rest[len(rounds) * count :]
    tile_count, edge = held.shape[0], held.shape[1]
    parts = in_sem.shape[0]
    per_part = tile_count // parts
    me = lax.axis_index("blk")
    loads = [
        pltpu.make_async_copy(
            tiles.at[pl.ds(part * per_part, per_part)],
            held.at[pl.ds(part * per_part, per_part)],
            in_sem.at[part],
        )
        for part in range(parts)
    ]
    for load in loads:
        load.start()
    for panel in range(count):
        used[panel] = 0

    @pl.loop(0, tile_count)
    def _(at):
        panel = panel_s[at]
        slot = used[panel]
        slot_tile[panel * slots + slot] = at
        used[panel] = slot + 1

    panels = panel_row[...]
    rows = max(count, 8)
    one_hot = (panels == lax.broadcasted_iota(jnp.int32, (rows, tile_count), 0)).astype(jnp.float32)
    earlier = (
        lax.broadcasted_iota(jnp.int32, (tile_count, tile_count), 0)
        < lax.broadcasted_iota(jnp.int32, (tile_count, tile_count), 1)
    ).astype(jnp.float32)
    before = jnp.dot(one_hot.astype(jnp.bfloat16), earlier.astype(jnp.bfloat16), preferred_element_type=jnp.float32)
    rank = jnp.sum(before * one_hot, axis=0, keepdims=True)
    rank_down = jnp.broadcast_to(rank, (tile_count, tile_count)).T
    at_slot = (
        rank_down == lax.broadcasted_iota(jnp.int32, (tile_count, tile_count), 1).astype(jnp.float32)
    ).astype(jnp.bfloat16)
    codes = one_hot * (code_row[...].astype(jnp.float32) + 1.0)
    label_rows[...] = jnp.dot(codes.astype(jnp.bfloat16), at_slot, preferred_element_type=jnp.float32) - 1.0
    label_copies = []
    for offset in order:
        panel = partner(me, offset, count)
        row = label_rows[pl.ds(panel, 1), :]
        label_blocks[offset] = jnp.broadcast_to(row, (LABEL_ROWS, tile_count)).astype(jnp.bfloat16)
        first_slots = rounds[0][1] - rounds[0][0]
        label_copies.append(
            pltpu.make_async_copy(
                label_blocks.at[offset],
                made[offset].at[pl.ds(first_slots * edge, LABEL_ROWS)],
                label_sem.at[offset],
            )
        )
        label_copies[-1].start()
    for load in loads:
        load.wait()
    for number, (low, high) in enumerate(rounds):
        for offset in order:
            panel = partner(me, offset, count)
            end = jnp.minimum(used[panel], high)
            target = made[number * count + offset]

            @pl.loop(low, jnp.maximum(end, low))
            def _(slot):
                pltpu.make_async_copy(
                    held.at[slot_tile[panel * slots + slot]],
                    target.at[pl.ds(pl.multiple_of((slot - low) * edge, edge), edge)],
                    out_sem,
                ).start()

    for copy in label_copies:
        copy.wait()
    pltpu.make_async_copy(tiles, held, out_sem).wait()


def pack(tiles, tile_panel, code, count, slots, rounds, order):
    tile_count, edge = tiles.shape[0], tiles.shape[1]
    shapes = []
    for number, (low, high) in enumerate(rounds):
        height = (high - low) * edge + (LABEL_ROWS if number == 0 else 0)
        shapes += [jax.ShapeDtypeStruct((height, edge), tiles.dtype)] * count
    return pl.pallas_call(
        functools.partial(pack_kernel, count, slots, rounds, order),
        out_shape=shapes,
        in_specs=[
            pl.BlockSpec(memory_space=pltpu.SMEM),
            pl.BlockSpec(memory_space=pltpu.VMEM),
            pl.BlockSpec(memory_space=pltpu.VMEM),
            pl.BlockSpec(memory_space=pl.ANY),
        ],
        out_specs=[pl.BlockSpec(memory_space=pl.ANY)] * len(shapes),
        scratch_shapes=[
            pltpu.VMEM(tiles.shape, tiles.dtype),
            pltpu.VMEM((max(count, 8), tile_count), jnp.float32),
            pltpu.VMEM((count, LABEL_ROWS, tile_count), jnp.bfloat16),
            pltpu.SMEM((count * slots,), jnp.int32),
            pltpu.SMEM((count,), jnp.int32),
            pltpu.SemaphoreType.DMA((4,)),
            pltpu.SemaphoreType.DMA,
            pltpu.SemaphoreType.DMA((count,)),
        ],
        name="pack",
    )(tile_panel, tile_panel.reshape(1, tile_count), code.reshape(1, tile_count), tiles)


def couple_kernel(count, slots, low, high, edge, order, first, last, labels, *rest):
    messages, rest = rest[:count], rest[count:]
    own, other, rest = rest[: STOPS // 2], rest[STOPS // 2 : STOPS], rest[STOPS:]
    if not first:
        total_in, rest = rest[0], rest[1:]
    result, held, basis, total, tile_sem, basis_sem, total_sem = rest
    core = lax.axis_index("blk") % 2
    height = (high - low) * edge
    copies = {}
    loads = []
    for at in range(STOPS // 2):
        for which, ref in ((core, own[at]), (1 - core, other[at])):
            loads.append(pltpu.make_async_copy(ref, basis.at[2 * at + which], basis_sem.at[len(loads)]))
            loads[-1].start()
    if not first:
        loads.append(pltpu.make_async_copy(total_in, total, total_sem))
        loads[-1].start()
    for offset in order:
        copies[offset] = pltpu.make_async_copy(
            messages[offset].at[pl.ds(0, height)], held.at[offset], tile_sem.at[offset]
        )
        copies[offset].start()
    if first:
        total[...] = jnp.zeros_like(total)
    for load in loads:
        load.wait()
    for offset in order:
        copies[offset].wait()

        @pl.loop(0, high - low)
        def _(slot):
            label = labels[offset * slots + low + slot]

            @pl.when(label >= 0)
            def _():
                row = label // STOPS
                stop = label % STOPS
                tile = held[offset, pl.ds(pl.multiple_of(slot * edge, edge), edge), :]
                at = pl.ds(pl.multiple_of(row * edge, edge), edge)
                total[at, :] += jnp.dot(
                    jnp.concatenate([tile, tile], axis=1), basis[stop], preferred_element_type=jnp.float32
                )

    if last:
        held_out = total[...].astype(jnp.bfloat16)
        result[...] = held_out
    else:
        out = pltpu.make_async_copy(total, result, total_sem)
        out.start()
        out.wait()


def couple(messages, labels, own, other, total, count, slots, low, high, edge, order, last):
    first = total is None
    operands = [labels, *messages, *own, *other] + ([] if first else [total])
    height = (high - low) * edge
    result = jax.ShapeDtypeStruct((PANEL, NOCC), jnp.bfloat16 if last else jnp.float32)
    return pl.pallas_call(
        functools.partial(couple_kernel, count, slots, low, high, edge, order, first, last),
        out_shape=result,
        in_specs=[pl.BlockSpec(memory_space=pltpu.SMEM)]
        + [pl.BlockSpec(memory_space=pl.ANY)] * (len(operands) - 1),
        out_specs=pl.BlockSpec(memory_space=pltpu.VMEM if last else pl.ANY),
        scratch_shapes=[
            pltpu.VMEM((count, height, edge), jnp.bfloat16),
            pltpu.VMEM((STOPS, 2 * edge, NOCC), jnp.bfloat16),
            pltpu.VMEM((PANEL, NOCC), jnp.float32),
            pltpu.SemaphoreType.DMA((count,)),
            pltpu.SemaphoreType.DMA((STOPS,)),
            pltpu.SemaphoreType.DMA,
        ],
        compiler_params=pltpu.CompilerParams(vmem_limit_bytes=48 * 1024 * 1024),
        name="couple_last" if last else "couple",
    )(*operands)


def per_device(integral_tiles, tile_panel, tile_row, tile_col, green_factor, window_start):
    count = lax.axis_size("blk")
    virt_count = lax.axis_size("virt")
    tile_count, edge = integral_tiles.shape[1], integral_tiles.shape[2]
    slots = max(2, 2 * tile_count // count)
    rounds = rounds_of(slots)
    order = offset_order(count)
    middle = STOPS // 2
    groups = virt_count // 2
    blk_at, virt_at = lax.axis_index("blk"), lax.axis_index("virt")
    everyone = [(block, virt) for block in range(count) for virt in range(virt_count)]

    window = lax.dynamic_slice_in_dim(green_factor, window_start[0], NOCC, 1)
    coarse = lax.reduce_precision(window, 8, 7)
    split = jnp.concatenate([coarse.astype(jnp.bfloat16), (window - coarse).astype(jnp.bfloat16)], axis=0)
    own = []
    for at in range(middle):
        pairs = []
        for block, virt in everyone:
            odd = virt % 2
            core = (block - odd) % 2
            panel = (block - odd - core - 2 * at + middle) % count
            pairs.append((block * virt_count + virt, (panel + core) * virt_count + virt))
        own.append(lax.ppermute(split, AXES, pairs))
    swap = [(block, block ^ 1) for block in range(count)]
    other = [lax.ppermute(array, "blk", swap) for array in own]

    code = tile_row[0] * STOPS + tile_col[0]
    packed = pack(integral_tiles[0], tile_panel[0, :, 0], code, count, slots, rounds, order)
    sent = [None] * len(packed)
    for number in range(len(rounds)):
        for offset in order:
            pairs = [
                (block * virt_count + virt, place_of(partner(block, offset, count), virt, virt_count))
                for block, virt in everyone
            ]
            sent[number * count + offset] = lax.ppermute(packed[number * count + offset], AXES, pairs)
    first_rows = (rounds[0][1] - rounds[0][0]) * edge
    labels = (
        jnp.stack([sent[offset][first_rows, :slots] for offset in range(count)]).astype(jnp.int32).reshape(-1)
    )
    total = None
    for number, (low, high) in enumerate(rounds):
        total = couple(
            sent[number * count : (number + 1) * count],
            labels,
            own,
            other,
            total,
            count,
            slots,
            low,
            high,
            edge,
            order,
            number == len(rounds) - 1,
        )

    mine = total
    theirs = lax.ppermute(mine, "blk", swap)
    piece = PANEL // virt_count
    contract = (((1,), (1,)), ((), ()))
    summed = None
    for message in range(groups):
        start = ((blk_at % 2) * groups + (virt_at // 2 + message) % groups) * piece
        part = sum(
            lax.dot_general(
                lax.dynamic_slice_in_dim(array, start, piece, 0), array, contract, preferred_element_type=jnp.float32
            )
            for array in (mine, theirs)
        )
        pairs = []
        for block, virt in everyone:
            panel = 2 * (block // 2) + virt % 2
            row = (block % 2) * groups + (virt // 2 + message) % groups
            pairs.append((block * virt_count + virt, panel * virt_count + row))
        came = lax.ppermute(part.astype(jnp.bfloat16), AXES, pairs).astype(jnp.float32)
        summed = came if summed is None else summed + came
    return summed * (-1.0 / math.sqrt(virt_count * NOCC))


def solution(mesh):
    return jax.shard_map(
        per_device,
        mesh=mesh,
        in_specs=(
            P("virt", "blk", None, None),
            P("virt", "blk", None),
            P("virt", "blk"),
            P("virt", "blk"),
            P("blk", None),
            P(),
        ),
        out_specs=P(("blk", "virt"), None),
        check_vma=False,
    )
```

```python
import functools
import math

import jax
import jax.numpy as jnp
from jax import lax
from jax.experimental import pallas as pl
from jax.experimental.pallas import tpu as pltpu
from jax.sharding import PartitionSpec as P


NOCC = 1024
STOPS = 8
PANEL = 1536
LABEL_ROWS = 16
AXES = ("blk", "virt")


def offset_order(count):
    def key(offset):
        chip = offset // 2
        return (bin(chip).count("1") or count, offset % 2, chip)

    return sorted(range(count), key=key)


def partner(block, offset, count):
    return block ^ offset if count & (count - 1) == 0 else (block + offset) % count


def place_of(panel, slab, virt_count):
    return (2 * (panel // 2) + slab % 2) * virt_count + 2 * (slab // 2) + panel % 2


def pack_kernel(count, slots, order, panel_s, panel_row, row_row, column_row, tiles, *rest):
    made, rest = rest[:count], rest[count:]
    held, label_rows, label_blocks, slot_tile, used, in_sem, out_sem, label_sem = rest
    tile_count, edge = held.shape[0], held.shape[1]
    parts = in_sem.shape[0]
    per_part = tile_count // parts
    me = lax.axis_index("blk")
    loads = [
        pltpu.make_async_copy(
            tiles.at[pl.ds(part * per_part, per_part)],
            held.at[pl.ds(part * per_part, per_part)],
            in_sem.at[part],
        )
        for part in range(parts)
    ]
    for load in loads:
        load.start()
    for panel in range(count):
        used[panel] = 0

    @pl.loop(0, tile_count)
    def _(at):
        panel = panel_s[at]
        slot = used[panel]
        slot_tile[panel * slots + slot] = at
        used[panel] = slot + 1

    panels = panel_row[...]
    square = (tile_count, tile_count)
    one_hot = (panels == lax.broadcasted_iota(jnp.int32, (max(count, 8), tile_count), 0)).astype(jnp.float32)
    earlier = lax.broadcasted_iota(jnp.int32, square, 0) < lax.broadcasted_iota(jnp.int32, square, 1)
    before = jnp.dot(
        one_hot.astype(jnp.bfloat16),
        earlier.astype(jnp.float32).astype(jnp.bfloat16),
        preferred_element_type=jnp.float32,
    )
    rank = jnp.sum(before * one_hot, axis=0, keepdims=True)
    at_slot = jnp.broadcast_to(rank, square).T == lax.broadcasted_iota(jnp.int32, square, 1).astype(jnp.float32)
    code = row_row[...] * STOPS + column_row[...]
    codes = one_hot * (code.astype(jnp.float32) + 1.0)
    label_rows[...] = (
        jnp.dot(
            codes.astype(jnp.bfloat16),
            at_slot.astype(jnp.float32).astype(jnp.bfloat16),
            preferred_element_type=jnp.float32,
        )
        - 1.0
    )
    label_copies = []
    for at, offset in enumerate(order):
        row = label_rows[pl.ds(partner(me, offset, count), 1), :]
        label_blocks[at] = jnp.broadcast_to(row, (LABEL_ROWS, tile_count)).astype(jnp.bfloat16)
        target = made[at].at[pl.ds(slots * edge, LABEL_ROWS)]
        label_copies.append(pltpu.make_async_copy(label_blocks.at[at], target, label_sem.at[at]))
        label_copies[-1].start()
    for load in loads:
        load.wait()
    for offset, target in zip(order, made):
        panel = partner(me, offset, count)

        @pl.loop(0, used[panel])
        def _(slot):
            pltpu.make_async_copy(
                held.at[slot_tile[panel * slots + slot]],
                target.at[pl.ds(pl.multiple_of(slot * edge, edge), edge)],
                out_sem,
            ).start()

    for copy in label_copies:
        copy.wait()
    pltpu.make_async_copy(tiles, held, out_sem).wait()


def pack(tiles, tile_panel, tile_row, tile_col, count, slots, order):
    tile_count, edge = tiles.shape[0], tiles.shape[1]
    shapes = [jax.ShapeDtypeStruct((slots * edge + LABEL_ROWS, edge), tiles.dtype)] * count
    return pl.pallas_call(
        functools.partial(pack_kernel, count, slots, order),
        out_shape=shapes,
        in_specs=[
            pl.BlockSpec(memory_space=pltpu.SMEM),
            pl.BlockSpec(memory_space=pltpu.VMEM),
            pl.BlockSpec(memory_space=pltpu.VMEM),
            pl.BlockSpec(memory_space=pltpu.VMEM),
            pl.BlockSpec(memory_space=pl.ANY),
        ],
        out_specs=[pl.BlockSpec(memory_space=pl.ANY)] * count,
        scratch_shapes=[
            pltpu.VMEM(tiles.shape, tiles.dtype),
            pltpu.VMEM((max(count, 8), tile_count), jnp.float32),
            pltpu.VMEM((count, LABEL_ROWS, tile_count), jnp.bfloat16),
            pltpu.SMEM((count * slots,), jnp.int32),
            pltpu.SMEM((count,), jnp.int32),
            pltpu.SemaphoreType.DMA((4,)),
            pltpu.SemaphoreType.DMA,
            pltpu.SemaphoreType.DMA((count,)),
        ],
        name="pack",
    )(tile_panel, tile_panel.reshape(1, tile_count), tile_row, tile_col, tiles)


def couple_kernel(count, slots, edge, *rest):
    messages, rest = rest[:count], rest[count:]
    coarse, fine, rest = rest[:STOPS], rest[STOPS : 2 * STOPS], rest[2 * STOPS :]
    result, held, basis, basis_rest, dense, made, rest = *rest[:6], rest[6:]
    label_blocks, label_rows, labels, tile_sem, basis_sem, label_sem, out_sem = rest
    core = lax.axis_index("blk") % 2
    loads = []
    for at in range(STOPS // 2):
        for half, stop in ((0, 2 * at + core), (STOPS // 2, 2 * at + 1 - core)):
            rows = pl.ds(pl.multiple_of(stop * edge, edge), edge)
            for ref, target in ((coarse[half + at], basis), (fine[half + at], basis_rest)):
                loads.append(pltpu.make_async_copy(ref, target.at[rows], basis_sem.at[len(loads)]))
    height = slots * edge
    label_loads = [
        pltpu.make_async_copy(ref.at[pl.ds(height, LABEL_ROWS)], label_blocks.at[at], label_sem.at[at])
        for at, ref in enumerate(messages)
    ]
    copies = [
        pltpu.make_async_copy(ref.at[pl.ds(0, height)], held.at[at], tile_sem.at[at]) for at, ref in enumerate(messages)
    ]
    for copy in label_loads + copies + loads:
        copy.start()
    dense[...] = jnp.zeros_like(dense)
    for at, copy in enumerate(label_loads):
        copy.wait()
        label_rows[pl.ds(at, 1), :] = label_blocks[at].astype(jnp.float32)[:1].astype(jnp.int32)
    copy = pltpu.make_async_copy(label_rows, labels, out_sem)
    copy.start()
    copy.wait()
    for at, copy in enumerate(copies):
        copy.wait()

        @pl.loop(0, slots)
        def _(slot):
            label = labels[at, slot]

            @pl.when(label >= 0)
            def _():
                rows = pl.ds(pl.multiple_of(label // STOPS * edge, edge), edge)
                columns = pl.ds(pl.multiple_of(label % STOPS * edge, edge), edge)
                tile = held[at, pl.ds(pl.multiple_of(slot * edge, edge), edge), :]
                dense[rows, columns] += tile.astype(jnp.float32)

    for load in loads:
        load.wait()
    step = PANEL // 4

    @pl.loop(0, 4)
    def _(at):
        rows = pl.ds(pl.multiple_of(at * step, step), step)
        value = dense[rows, :]
        high = value.astype(jnp.bfloat16)
        low = (value - high.astype(jnp.float32)).astype(jnp.bfloat16)
        sums = jnp.dot(high, basis_rest[...], preferred_element_type=jnp.float32)
        sums += jnp.dot(low, basis[...], preferred_element_type=jnp.float32)
        sums += jnp.dot(high, basis[...], preferred_element_type=jnp.float32)
        made[rows, :] = sums.astype(jnp.bfloat16)
        pltpu.make_async_copy(made.at[rows], result.at[rows], out_sem).start()

    pltpu.make_async_copy(made, result, out_sem).wait()


def couple(messages, coarse, fine, count, slots, edge):
    operands = [*messages, *coarse, *fine]
    return pl.pallas_call(
        functools.partial(couple_kernel, count, slots, edge),
        out_shape=jax.ShapeDtypeStruct((PANEL, NOCC), jnp.bfloat16),
        in_specs=[pl.BlockSpec(memory_space=pl.ANY)] * len(operands),
        out_specs=pl.BlockSpec(memory_space=pl.ANY),
        scratch_shapes=[
            pltpu.VMEM((count, slots * edge, edge), jnp.bfloat16),
            pltpu.VMEM((STOPS * edge, NOCC), jnp.bfloat16),
            pltpu.VMEM((STOPS * edge, NOCC), jnp.bfloat16),
            pltpu.VMEM((PANEL, STOPS * edge), jnp.float32),
            pltpu.VMEM((PANEL, NOCC), jnp.bfloat16),
            pltpu.VMEM((count, LABEL_ROWS, edge), jnp.bfloat16),
            pltpu.VMEM((count, edge), jnp.int32),
            pltpu.SMEM((count, edge), jnp.int32),
            pltpu.SemaphoreType.DMA((count,)),
            pltpu.SemaphoreType.DMA((2 * STOPS,)),
            pltpu.SemaphoreType.DMA((count,)),
            pltpu.SemaphoreType.DMA,
        ],
        name="couple",
    )(*operands)


STEPS = 32000.0


def coded(value):
    top = jnp.max(jnp.abs(value), axis=1, keepdims=True)
    scale_code = jnp.ceil(jnp.log2(jnp.maximum(top, 1e-30)) * 256.0)
    steps = jnp.round(value * (STEPS / jnp.exp2(scale_code / 256.0)))
    whole = jnp.concatenate([steps, jnp.broadcast_to(scale_code, (value.shape[0], 128))], axis=1)
    return whole.astype(jnp.int32).astype(jnp.int16)


def decoded(code, width):
    number = code.astype(jnp.int32).astype(jnp.float32)
    return number[:, :width] * (jnp.exp2(number[:, width : width + 1] / 256.0) / STEPS)


def per_device(integral_tiles, tile_panel, tile_row, tile_col, green_factor, window_start):
    count = lax.axis_size("blk")
    virt_count = lax.axis_size("virt")
    tile_count, edge = integral_tiles.shape[1], integral_tiles.shape[2]
    slots = max(2, 2 * tile_count // count)
    order = offset_order(count)
    middle = STOPS // 2
    groups = virt_count // 2
    blk_at, virt_at = lax.axis_index("blk"), lax.axis_index("virt")
    everyone = [(block, virt) for block in range(count) for virt in range(virt_count)]

    packed = pack(integral_tiles[0], tile_panel[0, :, 0], tile_row, tile_col, count, slots, order)
    sent = []
    for offset, message in zip(order, packed):
        pairs = [
            (block * virt_count + virt, place_of(partner(block, offset, count), virt, virt_count))
            for block, virt in everyone
        ]
        sent.append(lax.ppermute(message, AXES, pairs))

    window = coded(lax.dynamic_slice_in_dim(green_factor, window_start[0], NOCC, 1))
    own = []
    for at in range(middle):
        pairs = []
        for block, virt in everyone:
            odd = virt % 2
            core = (block - odd) % 2
            panel = (block - odd - core - 2 * at + middle) % count
            pairs.append((block * virt_count + virt, (panel + core) * virt_count + virt))
        own.append(lax.ppermute(window, AXES, pairs))
    swap = [(block, block ^ 1) for block in range(count)]
    other = [lax.ppermute(array, "blk", swap) for array in own]
    coarse, fine = [], []
    for part in own + other:
        part = decoded(part, NOCC)
        top = lax.reduce_precision(part, 8, 7)
        coarse.append(top.astype(jnp.bfloat16))
        fine.append((part - top).astype(jnp.bfloat16))
    total = couple(sent, coarse, fine, count, slots, edge)

    mine = total
    theirs = lax.ppermute(mine, "blk", swap)
    piece = PANEL // virt_count
    half = groups * piece
    contract = (((1,), (1,)), ((), ()))
    first_row = (blk_at % 2) * half
    mine_part = lax.optimization_barrier(
        lax.dot_general(
            lax.dynamic_slice_in_dim(mine, first_row, half, 0), mine, contract, preferred_element_type=jnp.float32
        )
    )
    summed = None
    for message in range(groups):
        start = (virt_at // 2 + message) % groups * piece
        part = lax.dynamic_slice_in_dim(mine_part, start, piece, 0) + lax.dot_general(
            lax.dynamic_slice_in_dim(theirs, first_row + start, piece, 0),
            theirs,
            contract,
            preferred_element_type=jnp.float32,
        )
        pairs = []
        for block, virt in everyone:
            panel = 2 * (block // 2) + virt % 2
            row = (block % 2) * groups + (virt // 2 + message) % groups
            pairs.append((block * virt_count + virt, panel * virt_count + row))
        came = lax.ppermute(part.astype(jnp.bfloat16), AXES, pairs).astype(jnp.float32)
        summed = came if summed is None else summed + came
    return summed * (-1.0 / math.sqrt(virt_count * NOCC))


def solution(mesh):
    return jax.shard_map(
        per_device,
        mesh=mesh,
        in_specs=(
            P("virt", "blk", None, None),
            P("virt", "blk", None),
            P("virt", "blk"),
            P("virt", "blk"),
            P("blk", None),
            P(),
        ),
        out_specs=P(("blk", "virt"), None),
        check_vma=False,
    )
```

```python
import functools
import math

import jax
import jax.numpy as jnp
from jax import lax
from jax.experimental import pallas as pl
from jax.experimental.pallas import tpu as pltpu
from jax.sharding import PartitionSpec as P


NOCC = 1024
STOPS = 8
PANEL = 1536
LABEL_ROWS = 16
AXES = ("blk", "virt")


def offset_order(count):
    def key(offset):
        chip = offset // 2
        return (bin(chip).count("1") or count, offset % 2, chip)

    return sorted(range(count), key=key)


def partner(block, offset, count):
    return block ^ offset if count & (count - 1) == 0 else (block + offset) % count


def place_of(panel, slab, virt_count):
    return (2 * (panel // 2) + slab % 2) * virt_count + 2 * (slab // 2) + panel % 2


def pack_kernel(count, slots, order, panel_s, panel_row, row_row, column_row, tiles, *rest):
    made, rest = rest[:count], rest[count:]
    held, label_rows, label_blocks, slot_tile, used, in_sem, out_sem, label_sem = rest
    tile_count, edge = held.shape[0], held.shape[1]
    parts = in_sem.shape[0]
    per_part = tile_count // parts
    me = lax.axis_index("blk")
    loads = [
        pltpu.make_async_copy(
            tiles.at[pl.ds(part * per_part, per_part)],
            held.at[pl.ds(part * per_part, per_part)],
            in_sem.at[part],
        )
        for part in range(parts)
    ]
    for load in loads:
        load.start()
    for panel in range(count):
        used[panel] = 0

    @pl.loop(0, tile_count)
    def _(at):
        panel = panel_s[at]
        slot = used[panel]
        slot_tile[panel * slots + slot] = at
        used[panel] = slot + 1

    panels = panel_row[...]
    square = (tile_count, tile_count)
    one_hot = (panels == lax.broadcasted_iota(jnp.int32, (max(count, 8), tile_count), 0)).astype(jnp.float32)
    earlier = lax.broadcasted_iota(jnp.int32, square, 0) < lax.broadcasted_iota(jnp.int32, square, 1)
    before = jnp.dot(
        one_hot.astype(jnp.bfloat16),
        earlier.astype(jnp.float32).astype(jnp.bfloat16),
        preferred_element_type=jnp.float32,
    )
    rank = jnp.sum(before * one_hot, axis=0, keepdims=True)
    at_slot = jnp.broadcast_to(rank, square).T == lax.broadcasted_iota(jnp.int32, square, 1).astype(jnp.float32)
    code = row_row[...] * STOPS + column_row[...]
    codes = one_hot * (code.astype(jnp.float32) + 1.0)
    label_rows[...] = (
        jnp.dot(
            codes.astype(jnp.bfloat16),
            at_slot.astype(jnp.float32).astype(jnp.bfloat16),
            preferred_element_type=jnp.float32,
        )
        - 1.0
    )
    label_copies = []
    for at, offset in enumerate(order):
        row = label_rows[pl.ds(partner(me, offset, count), 1), :]
        label_blocks[at] = jnp.broadcast_to(row, (LABEL_ROWS, tile_count)).astype(jnp.bfloat16)
        target = made[at].at[pl.ds(slots * edge, LABEL_ROWS)]
        label_copies.append(pltpu.make_async_copy(label_blocks.at[at], target, label_sem.at[at]))
        label_copies[-1].start()
    for load in loads:
        load.wait()
    for offset, target in zip(order, made):
        panel = partner(me, offset, count)

        @pl.loop(0, used[panel])
        def _(slot):
            pltpu.make_async_copy(
                held.at[slot_tile[panel * slots + slot]],
                target.at[pl.ds(pl.multiple_of(slot * edge, edge), edge)],
                out_sem,
            ).start()

    for copy in label_copies:
        copy.wait()
    pltpu.make_async_copy(tiles, held, out_sem).wait()


def pack(tiles, tile_panel, tile_row, tile_col, count, slots, order):
    tile_count, edge = tiles.shape[0], tiles.shape[1]
    shapes = [jax.ShapeDtypeStruct((slots * edge + LABEL_ROWS, edge), tiles.dtype)] * count
    return pl.pallas_call(
        functools.partial(pack_kernel, count, slots, order),
        out_shape=shapes,
        in_specs=[
            pl.BlockSpec(memory_space=pltpu.SMEM),
            pl.BlockSpec(memory_space=pltpu.VMEM),
            pl.BlockSpec(memory_space=pltpu.VMEM),
            pl.BlockSpec(memory_space=pltpu.VMEM),
            pl.BlockSpec(memory_space=pl.ANY),
        ],
        out_specs=[pl.BlockSpec(memory_space=pl.ANY)] * count,
        scratch_shapes=[
            pltpu.VMEM(tiles.shape, tiles.dtype),
            pltpu.VMEM((max(count, 8), tile_count), jnp.float32),
            pltpu.VMEM((count, LABEL_ROWS, tile_count), jnp.bfloat16),
            pltpu.SMEM((count * slots,), jnp.int32),
            pltpu.SMEM((count,), jnp.int32),
            pltpu.SemaphoreType.DMA((4,)),
            pltpu.SemaphoreType.DMA,
            pltpu.SemaphoreType.DMA((count,)),
        ],
        name="pack",
    )(tile_panel, tile_panel.reshape(1, tile_count), tile_row, tile_col, tiles)


def couple_kernel(count, slots, edge, *rest):
    messages, rest = rest[:count], rest[count:]
    coarse, fine, rest = rest[:STOPS], rest[STOPS : 2 * STOPS], rest[2 * STOPS :]
    result, held, basis, basis_rest, dense, made, rest = *rest[:6], rest[6:]
    label_blocks, label_rows, labels, tile_sem, basis_sem, label_sem, out_sem = rest
    core = lax.axis_index("blk") % 2
    loads = []
    for at in range(STOPS // 2):
        for half, stop in ((0, 2 * at + core), (STOPS // 2, 2 * at + 1 - core)):
            rows = pl.ds(pl.multiple_of(stop * edge, edge), edge)
            for ref, target in ((coarse[half + at], basis), (fine[half + at], basis_rest)):
                loads.append(pltpu.make_async_copy(ref, target.at[rows], basis_sem.at[len(loads)]))
    height = slots * edge
    label_loads = [
        pltpu.make_async_copy(ref.at[pl.ds(height, LABEL_ROWS)], label_blocks.at[at], label_sem.at[at])
        for at, ref in enumerate(messages)
    ]
    copies = [
        pltpu.make_async_copy(ref.at[pl.ds(0, height)], held.at[at], tile_sem.at[at]) for at, ref in enumerate(messages)
    ]
    for copy in label_loads + copies + loads:
        copy.start()
    dense[...] = jnp.zeros_like(dense)
    for at, copy in enumerate(label_loads):
        copy.wait()
        label_rows[pl.ds(at, 1), :] = label_blocks[at].astype(jnp.float32)[:1].astype(jnp.int32)
    copy = pltpu.make_async_copy(label_rows, labels, out_sem)
    copy.start()
    copy.wait()
    for at, copy in enumerate(copies):
        copy.wait()

        @pl.loop(0, slots)
        def _(slot):
            label = labels[at, slot]

            @pl.when(label >= 0)
            def _():
                rows = pl.ds(pl.multiple_of(label // STOPS * edge, edge), edge)
                columns = pl.ds(pl.multiple_of(label % STOPS * edge, edge), edge)
                tile = held[at, pl.ds(pl.multiple_of(slot * edge, edge), edge), :]
                dense[rows, columns] += tile.astype(jnp.float32)

    for load in loads:
        load.wait()
    step = PANEL // 4

    @pl.loop(0, 4)
    def _(at):
        rows = pl.ds(pl.multiple_of(at * step, step), step)
        value = dense[rows, :]
        high = value.astype(jnp.bfloat16)
        low = (value - high.astype(jnp.float32)).astype(jnp.bfloat16)
        sums = jnp.dot(high, basis_rest[...], preferred_element_type=jnp.float32)
        sums += jnp.dot(low, basis[...], preferred_element_type=jnp.float32)
        sums += jnp.dot(high, basis[...], preferred_element_type=jnp.float32)
        made[rows, :] = sums.astype(jnp.bfloat16)
        pltpu.make_async_copy(made.at[rows], result.at[rows], out_sem).start()

    pltpu.make_async_copy(made, result, out_sem).wait()


def couple(messages, coarse, fine, count, slots, edge):
    operands = [*messages, *coarse, *fine]
    return pl.pallas_call(
        functools.partial(couple_kernel, count, slots, edge),
        out_shape=jax.ShapeDtypeStruct((PANEL, NOCC), jnp.bfloat16),
        in_specs=[pl.BlockSpec(memory_space=pl.ANY)] * len(operands),
        out_specs=pl.BlockSpec(memory_space=pl.ANY),
        scratch_shapes=[
            pltpu.VMEM((count, slots * edge, edge), jnp.bfloat16),
            pltpu.VMEM((STOPS * edge, NOCC), jnp.bfloat16),
            pltpu.VMEM((STOPS * edge, NOCC), jnp.bfloat16),
            pltpu.VMEM((PANEL, STOPS * edge), jnp.float32),
            pltpu.VMEM((PANEL, NOCC), jnp.bfloat16),
            pltpu.VMEM((count, LABEL_ROWS, edge), jnp.bfloat16),
            pltpu.VMEM((count, edge), jnp.int32),
            pltpu.SMEM((count, edge), jnp.int32),
            pltpu.SemaphoreType.DMA((count,)),
            pltpu.SemaphoreType.DMA((2 * STOPS,)),
            pltpu.SemaphoreType.DMA((count,)),
            pltpu.SemaphoreType.DMA,
        ],
        compiler_params=pltpu.CompilerParams(vmem_limit_bytes=36 * 1024 * 1024),
        name="couple",
    )(*operands)


STEPS = 32000.0


def coded(value):
    top = jnp.max(jnp.abs(value), axis=1, keepdims=True)
    scale_code = jnp.ceil(jnp.log2(jnp.maximum(top, 1e-30)) * 256.0)
    steps = jnp.round(value * (STEPS / jnp.exp2(scale_code / 256.0)))
    whole = jnp.concatenate([steps, jnp.broadcast_to(scale_code, (value.shape[0], 128))], axis=1)
    return whole.astype(jnp.int32).astype(jnp.int16)


def decoded(code, width):
    number = code.astype(jnp.int32).astype(jnp.float32)
    return number[:, :width] * (jnp.exp2(number[:, width : width + 1] / 256.0) / STEPS)


def upper_blocks(count):
    return [(i, j) for i in range(count) for j in range(i, count)]


def rows_times_rows(left, right):
    return lax.dot_general(left, right, (((1,), (1,)), ((), ())), preferred_element_type=jnp.float32)


def load_halves(theirs, near, far, sems):
    half = near.shape[0]
    core = lax.axis_index("blk") % 2
    copies = []
    for at, (target, which) in enumerate(((near, core), (far, 1 - core))):
        rows = pl.ds(pl.multiple_of(which * half, half), half)
        copies.append(pltpu.make_async_copy(theirs.at[rows], target, sems.at[at]))
        copies[-1].start()
    return copies


def message_rows(near, message, piece):
    turn = (lax.axis_index("virt") // 2 + message) % 2
    return near[pl.ds(pl.multiple_of(turn * piece, piece), piece), :]


def own_join_kernel(piece, mine, between, *rest):
    acrosses, corners, (near, far, sems) = rest[:2], rest[2:4], rest[4:]
    copies = load_halves(mine, near, far, sems)
    copies[0].wait()
    between[...] = rows_times_rows(near[:piece, :], near[piece:, :])
    for message in range(2):
        rows = message_rows(near, message, piece)
        corners[message][...] = rows_times_rows(rows, rows)
    copies[1].wait()
    for message in range(2):
        acrosses[message][...] = rows_times_rows(message_rows(near, message, piece), far[...])


def own_join(mine, piece):
    half = mine.shape[0] // 2
    square, wide = (jax.ShapeDtypeStruct((piece, width), jnp.float32) for width in (piece, half))
    return pl.pallas_call(
        functools.partial(own_join_kernel, piece),
        out_shape=[square, wide, wide, square, square],
        in_specs=[pl.BlockSpec(memory_space=pl.ANY)],
        out_specs=[pl.BlockSpec(memory_space=pltpu.VMEM)] * 5,
        scratch_shapes=[
            pltpu.VMEM((half, mine.shape[1]), jnp.bfloat16),
            pltpu.VMEM((half, mine.shape[1]), jnp.bfloat16),
            pltpu.SemaphoreType.DMA((2,)),
        ],
        compiler_params=pltpu.CompilerParams(vmem_limit_bytes=20 * 1024 * 1024),
        name="own_join",
    )(mine)


def first_join_kernel(piece, theirs, between_part, across_part, between, across, near, far, held_b, held_a, sems):
    copies = load_halves(theirs, near, far, sems)
    for at, (ref, target) in enumerate(((between_part, held_b), (across_part, held_a))):
        copies.append(pltpu.make_async_copy(ref, target, sems.at[2 + at]))
        copies[-1].start()
    copies[0].wait()
    copies[2].wait()
    between[...] = (held_b[...] + rows_times_rows(near[:piece, :], near[piece:, :])).astype(jnp.bfloat16)
    copies[1].wait()
    copies[3].wait()
    across[...] = (held_a[...] + rows_times_rows(message_rows(near, 0, piece), far[...])).astype(jnp.bfloat16)


def second_join_kernel(piece, edge, theirs, across_part, *rest):
    corner_parts, (across, *corners), (near, far, held_a, *held_c, sems) = rest[:2], rest[2:5], rest[5:]
    copies = load_halves(theirs, near, far, sems)
    for at, (ref, target) in enumerate(zip((across_part, *corner_parts), (held_a, *held_c))):
        copies.append(pltpu.make_async_copy(ref, target, sems.at[2 + at]))
        copies[-1].start()
    copies[0].wait()
    for message in range(2):
        copies[3 + message].wait()
        rows = message_rows(near, message, piece)
        block = held_c[message][...] + rows_times_rows(rows, rows)
        for at, (i, j) in enumerate(upper_blocks(piece // edge)):
            corners[message][at * edge : (at + 1) * edge, :] = block[
                i * edge : (i + 1) * edge, j * edge : (j + 1) * edge
            ].astype(jnp.bfloat16)
    copies[1].wait()
    copies[2].wait()
    across[...] = (held_a[...] + rows_times_rows(message_rows(near, 1, piece), far[...])).astype(jnp.bfloat16)


def first_join(theirs, between_part, across_part, piece):
    half = theirs.shape[0] // 2
    return pl.pallas_call(
        functools.partial(first_join_kernel, piece),
        out_shape=[
            jax.ShapeDtypeStruct((piece, piece), jnp.bfloat16),
            jax.ShapeDtypeStruct((piece, half), jnp.bfloat16),
        ],
        in_specs=[pl.BlockSpec(memory_space=pl.ANY)] * 3,
        out_specs=[pl.BlockSpec(memory_space=pltpu.VMEM)] * 2,
        scratch_shapes=[
            pltpu.VMEM((half, theirs.shape[1]), jnp.bfloat16),
            pltpu.VMEM((half, theirs.shape[1]), jnp.bfloat16),
            pltpu.VMEM((piece, piece), jnp.float32),
            pltpu.VMEM((piece, half), jnp.float32),
            pltpu.SemaphoreType.DMA((4,)),
        ],
        compiler_params=pltpu.CompilerParams(vmem_limit_bytes=20 * 1024 * 1024),
        name="first_join",
    )(theirs, between_part, across_part)


def second_join(theirs, across_part, corner_part, other_corner_part, piece, edge):
    half = theirs.shape[0] // 2
    packed = (len(upper_blocks(piece // edge)) * edge, edge)
    return pl.pallas_call(
        functools.partial(second_join_kernel, piece, edge),
        out_shape=[
            jax.ShapeDtypeStruct((piece, half), jnp.bfloat16),
            jax.ShapeDtypeStruct(packed, jnp.bfloat16),
            jax.ShapeDtypeStruct(packed, jnp.bfloat16),
        ],
        in_specs=[pl.BlockSpec(memory_space=pl.ANY)] * 4,
        out_specs=[pl.BlockSpec(memory_space=pltpu.VMEM)] * 3,
        scratch_shapes=[
            pltpu.VMEM((half, theirs.shape[1]), jnp.bfloat16),
            pltpu.VMEM((half, theirs.shape[1]), jnp.bfloat16),
            pltpu.VMEM((piece, half), jnp.float32),
            pltpu.VMEM((piece, piece), jnp.float32),
            pltpu.VMEM((piece, piece), jnp.float32),
            pltpu.SemaphoreType.DMA((5,)),
        ],
        compiler_params=pltpu.CompilerParams(vmem_limit_bytes=20 * 1024 * 1024),
        name="second_join",
    )(theirs, across_part, corner_part, other_corner_part)


def assemble_kernel(piece, edge, factor, link, passed, side, other_side, corner, other_corner, result, *rest):
    made, rest = rest[0], rest[1:]
    held, sems, out_sem = rest[:6], rest[6], rest[7]
    half = 2 * piece
    virt = lax.axis_index("virt")
    order = (side, other_side, corner, other_corner, link, passed)
    copies = [pltpu.make_async_copy(ref, target, sems.at[at]) for at, (ref, target) in enumerate(zip(order, held))]
    for copy in copies:
        copy.start()
    side_h, other_side_h, corner_h, other_corner_h, link_h, passed_h = held

    def store(start, value):
        made[:, pl.ds(pl.multiple_of(start, edge), value.shape[1])] = value * factor

    def put(start):
        columns = pl.ds(pl.multiple_of(start, edge), half)
        copy = pltpu.make_async_copy(made.at[:, columns], result.at[:, columns], out_sem)
        copy.start()

    near, far = virt // 2 * half, (1 - virt // 2) * half
    copies[0].wait()
    copies[1].wait()
    store(far, side_h[...].astype(jnp.float32) + other_side_h[...].astype(jnp.float32))
    put(far)
    copies[2].wait()
    copies[3].wait()
    count = piece // edge
    blocks = {}
    for at, place in enumerate(upper_blocks(count)):
        rows = slice(at * edge, (at + 1) * edge)
        blocks[place] = corner_h[rows, :].astype(jnp.float32) + other_corner_h[rows, :].astype(jnp.float32)
    rows = [
        jnp.concatenate([blocks[i, j] if i <= j else blocks[j, i].T for j in range(count)], axis=1)
        for i in range(count)
    ]
    store(near + virt % 2 * piece, jnp.concatenate(rows, axis=0))
    copies[4].wait()
    copies[5].wait()

    @pl.when(virt % 2 == 0)
    def _():
        store(near + piece, link_h[...])

    @pl.when(virt % 2 == 1)
    def _():
        store(near, passed_h[...].astype(jnp.float32).T)

    put(near)
    pltpu.make_async_copy(made, result, out_sem).wait()


def assemble(link, passed, sides, corners, piece, edge, factor):
    operands = (link, passed, *sides, *corners)
    width = 4 * piece
    return pl.pallas_call(
        functools.partial(assemble_kernel, piece, edge, factor),
        out_shape=jax.ShapeDtypeStruct((piece, width), jnp.float32),
        in_specs=[pl.BlockSpec(memory_space=pl.ANY)] * len(operands),
        out_specs=pl.BlockSpec(memory_space=pl.ANY),
        scratch_shapes=[pltpu.VMEM((piece, width), jnp.float32)]
        + [pltpu.VMEM(array.shape, array.dtype) for array in (*sides, *corners, link, passed)]
        + [pltpu.SemaphoreType.DMA((6,)), pltpu.SemaphoreType.DMA],
        compiler_params=pltpu.CompilerParams(vmem_limit_bytes=20 * 1024 * 1024),
        name="assemble",
    )(*operands)


def per_device(integral_tiles, tile_panel, tile_row, tile_col, green_factor, window_start):
    count = lax.axis_size("blk")
    virt_count = lax.axis_size("virt")
    tile_count, edge = integral_tiles.shape[1], integral_tiles.shape[2]
    slots = max(2, 2 * tile_count // count)
    order = offset_order(count)
    middle = STOPS // 2
    everyone = [(block, virt) for block in range(count) for virt in range(virt_count)]

    packed = pack(integral_tiles[0], tile_panel[0, :, 0], tile_row, tile_col, count, slots, order)
    sent = []
    for offset, message in zip(order, packed):
        pairs = [
            (block * virt_count + virt, place_of(partner(block, offset, count), virt, virt_count))
            for block, virt in everyone
        ]
        sent.append(lax.ppermute(message, AXES, pairs))

    window = coded(lax.dynamic_slice_in_dim(green_factor, window_start[0], NOCC, 1))
    own = []
    for at in range(middle):
        pairs = []
        for block, virt in everyone:
            odd = virt % 2
            core = (block - odd) % 2
            panel = (block - odd - core - 2 * at + middle) % count
            pairs.append((block * virt_count + virt, (panel + core) * virt_count + virt))
        own.append(lax.ppermute(window, AXES, pairs))
    swap = [(block, block ^ 1) for block in range(count)]
    other = [lax.ppermute(array, "blk", swap) for array in own]
    coarse, fine = [], []
    for part in own + other:
        part = decoded(part, NOCC)
        top = lax.reduce_precision(part, 8, 7)
        coarse.append(top.astype(jnp.bfloat16))
        fine.append((part - top).astype(jnp.bfloat16))
    total = couple(sent, coarse, fine, count, slots, edge)

    mine = total
    theirs = lax.ppermute(mine, "blk", swap)
    piece = PANEL // virt_count
    between, *parts = own_join(mine, piece)
    between, across = first_join(theirs, between, parts[0], piece)
    other_across, *corners = second_join(theirs, *parts[1:], piece, edge)

    def sent_to(array, message=None, group=None):
        pairs = []
        for block, virt in everyone:
            row = block % 2 * 2 + (0 if message is None else (virt // 2 + message) % 2)
            if group is None or virt // 2 == group:
                pairs.append((block * virt_count + virt, (2 * (block // 2) + virt % 2) * virt_count + row))
        return lax.ppermute(array, AXES, pairs)

    links = [sent_to(between, group=group) for group in range(2)]
    sides = [sent_to(across, 0)]
    for message, corner in enumerate(corners):
        corners[message] = sent_to(corner, message)
    sides.append(sent_to(other_across, 1))
    on = [
        (block * virt_count + virt, block * virt_count + virt + 1)
        for block, virt in everyone
        if virt % 2 == 0
    ]
    link = links[0].astype(jnp.float32) + links[1].astype(jnp.float32)
    passed = lax.ppermute(link.astype(jnp.bfloat16), AXES, on)
    return assemble(link, passed, sides, corners, piece, edge, -1.0 / math.sqrt(virt_count * NOCC))


def solution(mesh):
    return jax.shard_map(
        per_device,
        mesh=mesh,
        in_specs=(
            P("virt", "blk", None, None),
            P("virt", "blk", None),
            P("virt", "blk"),
            P("virt", "blk"),
            P("blk", None),
            P(),
        ),
        out_specs=P(("blk", "virt"), None),
        check_vma=False,
    )
```

```python
import functools
import math

import jax
import jax.numpy as jnp
from jax import lax
from jax.experimental import pallas as pl
from jax.experimental.pallas import tpu as pltpu
from jax.sharding import PartitionSpec as P


NOCC = 1024
STOPS = 8
PANEL = 1536
LABEL_ROWS = 16
AXES = ("blk", "virt")


def offset_order(count):
    def key(offset):
        chip = offset // 2
        return (bin(chip).count("1") or count, offset % 2, chip)

    return sorted(range(count), key=key)


def partner(block, offset, count):
    return block ^ offset if count & (count - 1) == 0 else (block + offset) % count


def place_of(panel, slab, virt_count):
    return (2 * (panel // 2) + slab % 2) * virt_count + 2 * (slab // 2) + panel % 2


def pack_kernel(count, slots, order, panel_s, panel_row, row_row, column_row, tiles, *rest):
    made, rest = rest[:count], rest[count:]
    held, label_rows, label_blocks, slot_tile, used, in_sem, out_sem, label_sem = rest
    tile_count, edge = held.shape[0], held.shape[1]
    parts = in_sem.shape[0]
    per_part = tile_count // parts
    me = lax.axis_index("blk")
    loads = [
        pltpu.make_async_copy(
            tiles.at[pl.ds(part * per_part, per_part)],
            held.at[pl.ds(part * per_part, per_part)],
            in_sem.at[part],
        )
        for part in range(parts)
    ]
    for load in loads:
        load.start()
    for panel in range(count):
        used[panel] = 0

    @pl.loop(0, tile_count)
    def _(at):
        panel = panel_s[at]
        slot = used[panel]
        slot_tile[panel * slots + slot] = at
        used[panel] = slot + 1

    panels = panel_row[...]
    square = (tile_count, tile_count)
    one_hot = (panels == lax.broadcasted_iota(jnp.int32, (max(count, 8), tile_count), 0)).astype(jnp.float32)
    earlier = lax.broadcasted_iota(jnp.int32, square, 0) < lax.broadcasted_iota(jnp.int32, square, 1)
    before = jnp.dot(
        one_hot.astype(jnp.bfloat16),
        earlier.astype(jnp.float32).astype(jnp.bfloat16),
        preferred_element_type=jnp.float32,
    )
    rank = jnp.sum(before * one_hot, axis=0, keepdims=True)
    at_slot = jnp.broadcast_to(rank, square).T == lax.broadcasted_iota(jnp.int32, square, 1).astype(jnp.float32)
    code = row_row[...] * STOPS + column_row[...]
    codes = one_hot * (code.astype(jnp.float32) + 1.0)
    label_rows[...] = (
        jnp.dot(
            codes.astype(jnp.bfloat16),
            at_slot.astype(jnp.float32).astype(jnp.bfloat16),
            preferred_element_type=jnp.float32,
        )
        - 1.0
    )
    label_copies = []
    for at, offset in enumerate(order):
        row = label_rows[pl.ds(partner(me, offset, count), 1), :]
        label_blocks[at] = jnp.broadcast_to(row, (LABEL_ROWS, tile_count)).astype(jnp.bfloat16)
        target = made[at].at[pl.ds(slots * edge, LABEL_ROWS)]
        label_copies.append(pltpu.make_async_copy(label_blocks.at[at], target, label_sem.at[at]))
        label_copies[-1].start()
    for load in loads:
        load.wait()
    for offset, target in zip(order, made):
        panel = partner(me, offset, count)

        @pl.loop(0, used[panel])
        def _(slot):
            pltpu.make_async_copy(
                held.at[slot_tile[panel * slots + slot]],
                target.at[pl.ds(pl.multiple_of(slot * edge, edge), edge)],
                out_sem,
            ).start()

    for copy in label_copies:
        copy.wait()
    pltpu.make_async_copy(tiles, held, out_sem).wait()


def pack(tiles, tile_panel, tile_row, tile_col, count, slots, order):
    tile_count, edge = tiles.shape[0], tiles.shape[1]
    shapes = [jax.ShapeDtypeStruct((slots * edge + LABEL_ROWS, edge), tiles.dtype)] * count
    return pl.pallas_call(
        functools.partial(pack_kernel, count, slots, order),
        out_shape=shapes,
        in_specs=[
            pl.BlockSpec(memory_space=pltpu.SMEM),
            pl.BlockSpec(memory_space=pltpu.VMEM),
            pl.BlockSpec(memory_space=pltpu.VMEM),
            pl.BlockSpec(memory_space=pltpu.VMEM),
            pl.BlockSpec(memory_space=pl.ANY),
        ],
        out_specs=[pl.BlockSpec(memory_space=pl.ANY)] * count,
        scratch_shapes=[
            pltpu.VMEM(tiles.shape, tiles.dtype),
            pltpu.VMEM((max(count, 8), tile_count), jnp.float32),
            pltpu.VMEM((count, LABEL_ROWS, tile_count), jnp.bfloat16),
            pltpu.SMEM((count * slots,), jnp.int32),
            pltpu.SMEM((count,), jnp.int32),
            pltpu.SemaphoreType.DMA((4,)),
            pltpu.SemaphoreType.DMA,
            pltpu.SemaphoreType.DMA((count,)),
        ],
        name="pack",
    )(tile_panel, tile_panel.reshape(1, tile_count), tile_row, tile_col, tiles)


def couple_kernel(count, slots, edge, *rest):
    messages, rest = rest[:count], rest[count:]
    coarse, fine, rest = rest[:STOPS], rest[STOPS : 2 * STOPS], rest[2 * STOPS :]
    result, basis, basis_rest, dense, made, label_rows, labels, basis_sem, out_sem = rest
    core = lax.axis_index("blk") % 2
    loads = []
    for at in range(STOPS // 2):
        for half, stop in ((0, 2 * at + core), (STOPS // 2, 2 * at + 1 - core)):
            rows = pl.ds(pl.multiple_of(stop * edge, edge), edge)
            for ref, target in ((coarse[half + at], basis), (fine[half + at], basis_rest)):
                loads.append(pltpu.make_async_copy(ref, target.at[rows], basis_sem.at[len(loads)]))
    height = slots * edge
    for load in loads:
        load.start()
    for at, message in enumerate(messages):
        row = message[pl.ds(height, LABEL_ROWS), :].astype(jnp.float32)[:1]
        filled = jnp.sum((row >= 0.0).astype(jnp.float32), axis=1, keepdims=True)
        lane = lax.broadcasted_iota(jnp.int32, row.shape, 1)
        label_rows[pl.ds(at, 1), :] = jnp.where(lane == edge - 1, filled, row).astype(jnp.int32)
    copy = pltpu.make_async_copy(label_rows, labels, out_sem)
    copy.start()
    dense[...] = jnp.zeros_like(dense)
    copy.wait()
    together = min(4, slots)
    for at, message in enumerate(messages):

        @pl.loop(0, (labels[at, edge - 1] + together - 1) // together)
        def _(group):
            for inner in range(together):
                slot = group * together + inner
                label = labels[at, slot]

                @pl.when(label >= 0)
                def _():
                    rows = pl.ds(pl.multiple_of(label // STOPS * edge, edge), edge)
                    columns = pl.ds(pl.multiple_of(label % STOPS * edge, edge), edge)
                    tile = message[pl.ds(pl.multiple_of(slot * edge, edge), edge), :]
                    dense[rows, columns] += tile.astype(jnp.float32)

    for load in loads:
        load.wait()
    step = PANEL // 4
    for start in range(0, PANEL, step):
        rows = slice(start, start + step)
        value = dense[rows, :]
        high = value.astype(jnp.bfloat16)
        low = (value - high.astype(jnp.float32)).astype(jnp.bfloat16)
        sums = jnp.dot(high, basis_rest[...], preferred_element_type=jnp.float32)
        sums += jnp.dot(low, basis[...], preferred_element_type=jnp.float32)
        sums += jnp.dot(high, basis[...], preferred_element_type=jnp.float32)
        made[rows, :] = sums.astype(jnp.bfloat16)
        pltpu.make_async_copy(made.at[rows], result.at[rows], out_sem).start()
    pltpu.make_async_copy(made, result, out_sem).wait()


def couple(messages, coarse, fine, count, slots, edge):
    operands = [*messages, *coarse, *fine]
    return pl.pallas_call(
        functools.partial(couple_kernel, count, slots, edge),
        out_shape=jax.ShapeDtypeStruct((PANEL, NOCC), jnp.bfloat16),
        in_specs=[pl.BlockSpec(memory_space=pltpu.VMEM)] * count
        + [pl.BlockSpec(memory_space=pl.ANY)] * (2 * STOPS),
        out_specs=pl.BlockSpec(memory_space=pl.ANY),
        scratch_shapes=[
            pltpu.VMEM((STOPS * edge, NOCC), jnp.bfloat16),
            pltpu.VMEM((STOPS * edge, NOCC), jnp.bfloat16),
            pltpu.VMEM((PANEL, STOPS * edge), jnp.float32),
            pltpu.VMEM((PANEL, NOCC), jnp.bfloat16),
            pltpu.VMEM((count, edge), jnp.int32),
            pltpu.SMEM((count, edge), jnp.int32),
            pltpu.SemaphoreType.DMA((2 * STOPS,)),
            pltpu.SemaphoreType.DMA,
        ],
        compiler_params=pltpu.CompilerParams(vmem_limit_bytes=36 * 1024 * 1024),
        name="couple",
    )(*operands)


STEPS = 32000.0


def window_kernel(start, green, result, held, sem):
    wide = held.shape[1]
    first = jnp.minimum(start[0] // 128 * 128, green.shape[1] - wide)
    copy = pltpu.make_async_copy(green.at[:, pl.ds(pl.multiple_of(first, 128), wide)], held, sem)
    copy.start()
    copy.wait()
    value = pltpu.roll(held[...], (wide + first - start[0]) % wide, 1)[:, :NOCC]
    top = jnp.max(jnp.abs(value), axis=1, keepdims=True)
    scale_code = jnp.ceil(jnp.log2(jnp.maximum(top, 1e-30)) * 256.0)
    steps = jnp.round(value * (STEPS / jnp.exp2(scale_code * (1.0 / 256.0))))
    result[:, :NOCC] = steps.astype(jnp.int32).astype(jnp.int16)
    result[:, NOCC:] = jnp.broadcast_to(scale_code, (value.shape[0], 128)).astype(jnp.int32).astype(jnp.int16)


def coded_window(green, start):
    rows = green.shape[0]
    return pl.pallas_call(
        window_kernel,
        out_shape=jax.ShapeDtypeStruct((rows, NOCC + 128), jnp.int16),
        in_specs=[pl.BlockSpec(memory_space=pltpu.SMEM), pl.BlockSpec(memory_space=pl.ANY)],
        out_specs=pl.BlockSpec(memory_space=pltpu.VMEM),
        scratch_shapes=[pltpu.VMEM((rows, NOCC + 128), jnp.float32), pltpu.SemaphoreType.DMA],
        name="window",
    )(start, green)


def decoded(code, width):
    number = code.astype(jnp.int32).astype(jnp.float32)
    return number[:, :width] * (jnp.exp2(number[:, width : width + 1] / 256.0) / STEPS)


def upper_blocks(count):
    return [(i, j) for i in range(count) for j in range(i, count)]


def rows_times_rows(left, right):
    return lax.dot_general(left, right, (((1,), (1,)), ((), ())), preferred_element_type=jnp.float32)


def load_halves(theirs, near, far, sems):
    half = near.shape[0]
    core = lax.axis_index("blk") % 2
    copies = []
    for at, (target, which) in enumerate(((near, core), (far, 1 - core))):
        rows = pl.ds(pl.multiple_of(which * half, half), half)
        copies.append(pltpu.make_async_copy(theirs.at[rows], target, sems.at[at]))
        copies[-1].start()
    return copies


def message_rows(near, message, piece):
    turn = (lax.axis_index("virt") // 2 + message) % 2
    return near[pl.ds(pl.multiple_of(turn * piece, piece), piece), :]


def own_join_kernel(piece, mine, between, *rest):
    acrosses, corners, (near, far, sems) = rest[:2], rest[2:4], rest[4:]
    copies = load_halves(mine, near, far, sems)
    copies[0].wait()
    between[...] = rows_times_rows(near[:piece, :], near[piece:, :])
    for message in range(2):
        rows = message_rows(near, message, piece)
        corners[message][...] = rows_times_rows(rows, rows)
    copies[1].wait()
    for message in range(2):
        acrosses[message][...] = rows_times_rows(message_rows(near, message, piece), far[...])


def own_join(mine, piece):
    half = mine.shape[0] // 2
    square, wide = (jax.ShapeDtypeStruct((piece, width), jnp.float32) for width in (piece, half))
    return pl.pallas_call(
        functools.partial(own_join_kernel, piece),
        out_shape=[square, wide, wide, square, square],
        in_specs=[pl.BlockSpec(memory_space=pl.ANY)],
        out_specs=[pl.BlockSpec(memory_space=pltpu.VMEM)] * 5,
        scratch_shapes=[
            pltpu.VMEM((half, mine.shape[1]), jnp.bfloat16),
            pltpu.VMEM((half, mine.shape[1]), jnp.bfloat16),
            pltpu.SemaphoreType.DMA((2,)),
        ],
        compiler_params=pltpu.CompilerParams(vmem_limit_bytes=20 * 1024 * 1024),
        name="own_join",
    )(mine)


def first_join_kernel(piece, theirs, between_part, across_part, between, across, near, far, held_b, held_a, sems):
    copies = load_halves(theirs, near, far, sems)
    for at, (ref, target) in enumerate(((between_part, held_b), (across_part, held_a))):
        copies.append(pltpu.make_async_copy(ref, target, sems.at[2 + at]))
        copies[-1].start()
    copies[0].wait()
    copies[2].wait()
    between[...] = (held_b[...] + rows_times_rows(near[:piece, :], near[piece:, :])).astype(jnp.bfloat16)
    copies[1].wait()
    copies[3].wait()
    across[...] = (held_a[...] + rows_times_rows(message_rows(near, 0, piece), far[...])).astype(jnp.bfloat16)


def second_join_kernel(piece, edge, theirs, across_part, *rest):
    corner_parts, (across, *corners), (near, far, held_a, *held_c, sems) = rest[:2], rest[2:5], rest[5:]
    copies = load_halves(theirs, near, far, sems)
    for at, (ref, target) in enumerate(zip((across_part, *corner_parts), (held_a, *held_c))):
        copies.append(pltpu.make_async_copy(ref, target, sems.at[2 + at]))
        copies[-1].start()
    copies[0].wait()
    for message in range(2):
        copies[3 + message].wait()
        rows = message_rows(near, message, piece)
        block = held_c[message][...] + rows_times_rows(rows, rows)
        for at, (i, j) in enumerate(upper_blocks(piece // edge)):
            corners[message][at * edge : (at + 1) * edge, :] = block[
                i * edge : (i + 1) * edge, j * edge : (j + 1) * edge
            ].astype(jnp.bfloat16)
    copies[1].wait()
    copies[2].wait()
    across[...] = (held_a[...] + rows_times_rows(message_rows(near, 1, piece), far[...])).astype(jnp.bfloat16)


def first_join(theirs, between_part, across_part, piece):
    half = theirs.shape[0] // 2
    return pl.pallas_call(
        functools.partial(first_join_kernel, piece),
        out_shape=[
            jax.ShapeDtypeStruct((piece, piece), jnp.bfloat16),
            jax.ShapeDtypeStruct((piece, half), jnp.bfloat16),
        ],
        in_specs=[pl.BlockSpec(memory_space=pl.ANY)] * 3,
        out_specs=[pl.BlockSpec(memory_space=pltpu.VMEM)] * 2,
        scratch_shapes=[
            pltpu.VMEM((half, theirs.shape[1]), jnp.bfloat16),
            pltpu.VMEM((half, theirs.shape[1]), jnp.bfloat16),
            pltpu.VMEM((piece, piece), jnp.float32),
            pltpu.VMEM((piece, half), jnp.float32),
            pltpu.SemaphoreType.DMA((4,)),
        ],
        compiler_params=pltpu.CompilerParams(vmem_limit_bytes=20 * 1024 * 1024),
        name="first_join",
    )(theirs, between_part, across_part)


def second_join(theirs, across_part, corner_part, other_corner_part, piece, edge):
    half = theirs.shape[0] // 2
    packed = (len(upper_blocks(piece // edge)) * edge, edge)
    return pl.pallas_call(
        functools.partial(second_join_kernel, piece, edge),
        out_shape=[
            jax.ShapeDtypeStruct((piece, half), jnp.bfloat16),
            jax.ShapeDtypeStruct(packed, jnp.bfloat16),
            jax.ShapeDtypeStruct(packed, jnp.bfloat16),
        ],
        in_specs=[pl.BlockSpec(memory_space=pl.ANY)] * 4,
        out_specs=[pl.BlockSpec(memory_space=pltpu.VMEM)] * 3,
        scratch_shapes=[
            pltpu.VMEM((half, theirs.shape[1]), jnp.bfloat16),
            pltpu.VMEM((half, theirs.shape[1]), jnp.bfloat16),
            pltpu.VMEM((piece, half), jnp.float32),
            pltpu.VMEM((piece, piece), jnp.float32),
            pltpu.VMEM((piece, piece), jnp.float32),
            pltpu.SemaphoreType.DMA((5,)),
        ],
        compiler_params=pltpu.CompilerParams(vmem_limit_bytes=20 * 1024 * 1024),
        name="second_join",
    )(theirs, across_part, corner_part, other_corner_part)


def near_kernel(piece, edge, factor, link, passed, corner, other_corner, result, made, *rest):
    held, sems, out_sem = rest[:4], rest[4], rest[5]
    half = 2 * piece
    virt = lax.axis_index("virt")
    operands = (corner, other_corner, link, passed)
    copies = [pltpu.make_async_copy(ref, target, sems.at[at]) for at, (ref, target) in enumerate(zip(operands, held))]
    for copy in copies:
        copy.start()
    corner_h, other_corner_h, link_h, passed_h = held

    def store(start, value):
        made[:, pl.ds(pl.multiple_of(start, edge), piece)] = value * factor

    copies[0].wait()
    copies[1].wait()
    count = piece // edge
    blocks = {}
    for at, place in enumerate(upper_blocks(count)):
        rows = slice(at * edge, (at + 1) * edge)
        blocks[place] = corner_h[rows, :].astype(jnp.float32) + other_corner_h[rows, :].astype(jnp.float32)
    rows = [
        jnp.concatenate([blocks[i, j] if i <= j else blocks[j, i].T for j in range(count)], axis=1)
        for i in range(count)
    ]
    store(virt % 2 * piece, jnp.concatenate(rows, axis=0))
    copies[2].wait()
    copies[3].wait()

    @pl.when(virt % 2 == 0)
    def _():
        store(piece, link_h[...])

    @pl.when(virt % 2 == 1)
    def _():
        store(0, passed_h[...].astype(jnp.float32).T)

    columns = pl.ds(pl.multiple_of(virt // 2 * half, half), half)
    copy = pltpu.make_async_copy(made, result.at[:, columns], out_sem)
    copy.start()
    copy.wait()


def far_kernel(factor, begun, side, other_side, result, made, side_h, other_side_h, sems):
    half = made.shape[1]
    copies = [
        pltpu.make_async_copy(ref, target, sems.at[at])
        for at, (ref, target) in enumerate(((side, side_h), (other_side, other_side_h)))
    ]
    for copy in copies:
        copy.start()
    for copy in copies:
        copy.wait()
    made[...] = (side_h[...].astype(jnp.float32) + other_side_h[...].astype(jnp.float32)) * factor
    columns = pl.ds(pl.multiple_of((1 - lax.axis_index("virt") // 2) * half, half), half)
    copy = pltpu.make_async_copy(made, result.at[:, columns], sems.at[2])
    copy.start()
    copy.wait()


def assemble(link, passed, sides, corners, piece, edge, factor):
    half = 2 * piece
    result = jax.ShapeDtypeStruct((piece, 2 * half), jnp.float32)
    anywhere = pl.BlockSpec(memory_space=pl.ANY)
    begun = pl.pallas_call(
        functools.partial(near_kernel, piece, edge, factor),
        out_shape=result,
        in_specs=[anywhere] * 4,
        out_specs=anywhere,
        scratch_shapes=[pltpu.VMEM((piece, half), jnp.float32)]
        + [pltpu.VMEM(array.shape, array.dtype) for array in (*corners, link, passed)]
        + [pltpu.SemaphoreType.DMA((4,)), pltpu.SemaphoreType.DMA],
        compiler_params=pltpu.CompilerParams(vmem_limit_bytes=20 * 1024 * 1024),
        name="near_half",
    )(link, passed, *corners)
    return pl.pallas_call(
        functools.partial(far_kernel, factor),
        out_shape=result,
        in_specs=[anywhere] * 3,
        out_specs=anywhere,
        input_output_aliases={0: 0},
        scratch_shapes=[pltpu.VMEM((piece, half), jnp.float32)]
        + [pltpu.VMEM(array.shape, array.dtype) for array in sides]
        + [pltpu.SemaphoreType.DMA((3,))],
        compiler_params=pltpu.CompilerParams(vmem_limit_bytes=20 * 1024 * 1024),
        name="far_half",
    )(begun, *sides)


def per_device(integral_tiles, tile_panel, tile_row, tile_col, green_factor, window_start):
    count = lax.axis_size("blk")
    virt_count = lax.axis_size("virt")
    tile_count, edge = integral_tiles.shape[1], integral_tiles.shape[2]
    slots = max(2, 2 * tile_count // count)
    order = offset_order(count)
    middle = STOPS // 2
    everyone = [(block, virt) for block in range(count) for virt in range(virt_count)]

    packed = pack(integral_tiles[0], tile_panel[0, :, 0], tile_row, tile_col, count, slots, order)
    sent = []
    for offset, message in zip(order, packed):
        pairs = [
            (block * virt_count + virt, place_of(partner(block, offset, count), virt, virt_count))
            for block, virt in everyone
        ]
        sent.append(lax.ppermute(message, AXES, pairs))

    window = coded_window(green_factor, window_start)
    own = []
    for at in range(middle):
        pairs = []
        for block, virt in everyone:
            odd = virt % 2
            core = (block - odd) % 2
            panel = (block - odd - core - 2 * at + middle) % count
            pairs.append((block * virt_count + virt, (panel + core) * virt_count + virt))
        own.append(lax.ppermute(window, AXES, pairs))
    swap = [(block, block ^ 1) for block in range(count)]
    other = [lax.ppermute(array, "blk", swap) for array in own]
    coarse, fine = [], []
    for part in own + other:
        part = decoded(part, NOCC)
        top = lax.reduce_precision(part, 8, 7)
        coarse.append(top.astype(jnp.bfloat16))
        fine.append((part - top).astype(jnp.bfloat16))
    total = couple(sent, coarse, fine, count, slots, edge)

    mine = total
    theirs = lax.ppermute(mine, "blk", swap)
    piece = PANEL // virt_count
    between, *parts = own_join(mine, piece)
    between, across = first_join(theirs, between, parts[0], piece)
    other_across, *corners = second_join(theirs, *parts[1:], piece, edge)

    def sent_to(array, message=None, group=None):
        pairs = []
        for block, virt in everyone:
            row = block % 2 * 2 + (0 if message is None else (virt // 2 + message) % 2)
            if group is None or virt // 2 == group:
                pairs.append((block * virt_count + virt, (2 * (block // 2) + virt % 2) * virt_count + row))
        return lax.ppermute(array, AXES, pairs)

    links = [sent_to(between, group=group) for group in range(2)]
    sides = [sent_to(across, 0)]
    for message, corner in enumerate(corners):
        corners[message] = sent_to(corner, message)
    sides.append(sent_to(other_across, 1))
    on = [
        (block * virt_count + virt, block * virt_count + virt + 1)
        for block, virt in everyone
        if virt % 2 == 0
    ]
    link = links[0].astype(jnp.float32) + links[1].astype(jnp.float32)
    passed = lax.ppermute(link.astype(jnp.bfloat16), AXES, on)
    return assemble(link, passed, sides, corners, piece, edge, -1.0 / math.sqrt(virt_count * NOCC))


def solution(mesh):
    return jax.shard_map(
        per_device,
        mesh=mesh,
        in_specs=(
            P("virt", "blk", None, None),
            P("virt", "blk", None),
            P("virt", "blk"),
            P("virt", "blk"),
            P("blk", None),
            P(),
        ),
        out_specs=P(("blk", "virt"), None),
        check_vma=False,
    )
```

```python
import functools
import math

import jax
import jax.numpy as jnp
from jax import lax
from jax.experimental import pallas as pl
from jax.experimental.pallas import tpu as pltpu
from jax.sharding import PartitionSpec as P


NOCC = 1024
STOPS = 8
PANEL = 1536
LABEL_ROWS = 16
AXES = ("blk", "virt")


def offset_order(count):
    def key(offset):
        chip = offset // 2
        return (bin(chip).count("1") or count, offset % 2, chip)

    return sorted(range(count), key=key)


def partner(block, offset, count):
    return block ^ offset if count & (count - 1) == 0 else (block + offset) % count


def place_of(panel, slab, virt_count):
    return (2 * (panel // 2) + slab % 2) * virt_count + 2 * (slab // 2) + panel % 2


def pack_kernel(count, slots, order, panel_s, panel_row, row_row, column_row, tiles, *rest):
    made, rest = rest[:count], rest[count:]
    held, label_rows, label_blocks, slot_tile, used, in_sem, out_sem, label_sem = rest
    tile_count, edge = held.shape[0], held.shape[1]
    parts = in_sem.shape[0]
    per_part = tile_count // parts
    me = lax.axis_index("blk")
    loads = [
        pltpu.make_async_copy(
            tiles.at[pl.ds(part * per_part, per_part)],
            held.at[pl.ds(part * per_part, per_part)],
            in_sem.at[part],
        )
        for part in range(parts)
    ]
    for load in loads:
        load.start()
    for panel in range(count):
        used[panel] = 0

    @pl.loop(0, tile_count)
    def _(at):
        panel = panel_s[at]
        slot = used[panel]
        slot_tile[panel * slots + slot] = at
        used[panel] = slot + 1

    panels = panel_row[...]
    square = (tile_count, tile_count)
    one_hot = (panels == lax.broadcasted_iota(jnp.int32, (max(count, 8), tile_count), 0)).astype(jnp.float32)
    earlier = lax.broadcasted_iota(jnp.int32, square, 0) < lax.broadcasted_iota(jnp.int32, square, 1)
    before = jnp.dot(
        one_hot.astype(jnp.bfloat16),
        earlier.astype(jnp.float32).astype(jnp.bfloat16),
        preferred_element_type=jnp.float32,
    )
    rank = jnp.sum(before * one_hot, axis=0, keepdims=True)
    at_slot = jnp.broadcast_to(rank, square).T == lax.broadcasted_iota(jnp.int32, square, 1).astype(jnp.float32)
    code = row_row[...] * STOPS + column_row[...]
    codes = one_hot * (code.astype(jnp.float32) + 1.0)
    label_rows[...] = (
        jnp.dot(
            codes.astype(jnp.bfloat16),
            at_slot.astype(jnp.float32).astype(jnp.bfloat16),
            preferred_element_type=jnp.float32,
        )
        - 1.0
    )
    label_copies = []
    for at, offset in enumerate(order):
        row = label_rows[pl.ds(partner(me, offset, count), 1), :]
        label_blocks[at] = jnp.broadcast_to(row, (LABEL_ROWS, tile_count)).astype(jnp.bfloat16)
        target = made[at].at[pl.ds(slots * edge, LABEL_ROWS)]
        label_copies.append(pltpu.make_async_copy(label_blocks.at[at], target, label_sem.at[at]))
        label_copies[-1].start()
    for load in loads:
        load.wait()
    for offset, target in zip(order, made):
        panel = partner(me, offset, count)

        @pl.loop(0, used[panel])
        def _(slot):
            pltpu.make_async_copy(
                held.at[slot_tile[panel * slots + slot]],
                target.at[pl.ds(pl.multiple_of(slot * edge, edge), edge)],
                out_sem,
            ).start()

    for copy in label_copies:
        copy.wait()
    pltpu.make_async_copy(tiles, held, out_sem).wait()


def pack(tiles, tile_panel, tile_row, tile_col, count, slots, order):
    tile_count, edge = tiles.shape[0], tiles.shape[1]
    shapes = [jax.ShapeDtypeStruct((slots * edge + LABEL_ROWS, edge), tiles.dtype)] * count
    return pl.pallas_call(
        functools.partial(pack_kernel, count, slots, order),
        out_shape=shapes,
        in_specs=[
            pl.BlockSpec(memory_space=pltpu.SMEM),
            pl.BlockSpec(memory_space=pltpu.VMEM),
            pl.BlockSpec(memory_space=pltpu.VMEM),
            pl.BlockSpec(memory_space=pltpu.VMEM),
            pl.BlockSpec(memory_space=pl.ANY),
        ],
        out_specs=[pl.BlockSpec(memory_space=pl.ANY)] * count,
        scratch_shapes=[
            pltpu.VMEM(tiles.shape, tiles.dtype),
            pltpu.VMEM((max(count, 8), tile_count), jnp.float32),
            pltpu.VMEM((count, LABEL_ROWS, tile_count), jnp.bfloat16),
            pltpu.SMEM((count * slots,), jnp.int32),
            pltpu.SMEM((count,), jnp.int32),
            pltpu.SemaphoreType.DMA((4,)),
            pltpu.SemaphoreType.DMA,
            pltpu.SemaphoreType.DMA((count,)),
        ],
        name="pack",
    )(tile_panel, tile_panel.reshape(1, tile_count), tile_row, tile_col, tiles)


def couple_kernel(count, slots, edge, *rest):
    messages, rest = rest[:count], rest[count:]
    coarse, fine, rest = rest[:STOPS], rest[STOPS : 2 * STOPS], rest[2 * STOPS :]
    result, basis, basis_rest, dense, made, label_rows, labels, basis_sem, out_sem = rest
    core = lax.axis_index("blk") % 2
    loads = []
    for at in range(STOPS // 2):
        for half, stop in ((0, 2 * at + core), (STOPS // 2, 2 * at + 1 - core)):
            rows = pl.ds(pl.multiple_of(stop * edge, edge), edge)
            for ref, target in ((coarse[half + at], basis), (fine[half + at], basis_rest)):
                loads.append(pltpu.make_async_copy(ref, target.at[rows], basis_sem.at[len(loads)]))
    height = slots * edge
    for load in loads:
        load.start()
    for at, message in enumerate(messages):
        row = message[pl.ds(height, LABEL_ROWS), :].astype(jnp.float32)[:1]
        filled = jnp.sum((row >= 0.0).astype(jnp.float32), axis=1, keepdims=True)
        lane = lax.broadcasted_iota(jnp.int32, row.shape, 1)
        label_rows[pl.ds(at, 1), :] = jnp.where(lane == edge - 1, filled, row).astype(jnp.int32)
    copy = pltpu.make_async_copy(label_rows, labels, out_sem)
    copy.start()
    dense[...] = jnp.zeros_like(dense)
    copy.wait()
    together = min(4, slots)
    for at, message in enumerate(messages):

        @pl.loop(0, (labels[at, edge - 1] + together - 1) // together)
        def _(group):
            for inner in range(together):
                slot = group * together + inner
                label = labels[at, slot]

                @pl.when(label >= 0)
                def _():
                    rows = pl.ds(pl.multiple_of(label // STOPS * edge, edge), edge)
                    columns = pl.ds(pl.multiple_of(label % STOPS * edge, edge), edge)
                    tile = message[pl.ds(pl.multiple_of(slot * edge, edge), edge), :]
                    dense[rows, columns] += tile.astype(jnp.float32)

    for load in loads:
        load.wait()
    step = PANEL // 4
    for start in range(0, PANEL, step):
        rows = slice(start, start + step)
        value = dense[rows, :]
        high = value.astype(jnp.bfloat16)
        low = (value - high.astype(jnp.float32)).astype(jnp.bfloat16)
        sums = jnp.dot(high, basis_rest[...], preferred_element_type=jnp.float32)
        sums += jnp.dot(low, basis[...], preferred_element_type=jnp.float32)
        sums += jnp.dot(high, basis[...], preferred_element_type=jnp.float32)
        made[rows, :] = sums.astype(jnp.bfloat16)
        pltpu.make_async_copy(made.at[rows], result.at[rows], out_sem).start()
    pltpu.make_async_copy(made, result, out_sem).wait()


def couple(messages, coarse, fine, count, slots, edge):
    operands = [*messages, *coarse, *fine]
    return pl.pallas_call(
        functools.partial(couple_kernel, count, slots, edge),
        out_shape=jax.ShapeDtypeStruct((PANEL, NOCC), jnp.bfloat16),
        in_specs=[pl.BlockSpec(memory_space=pltpu.VMEM)] * count
        + [pl.BlockSpec(memory_space=pl.ANY)] * (2 * STOPS),
        out_specs=pl.BlockSpec(memory_space=pl.ANY),
        scratch_shapes=[
            pltpu.VMEM((STOPS * edge, NOCC), jnp.bfloat16),
            pltpu.VMEM((STOPS * edge, NOCC), jnp.bfloat16),
            pltpu.VMEM((PANEL, STOPS * edge), jnp.float32),
            pltpu.VMEM((PANEL, NOCC), jnp.bfloat16),
            pltpu.VMEM((count, edge), jnp.int32),
            pltpu.SMEM((count, edge), jnp.int32),
            pltpu.SemaphoreType.DMA((2 * STOPS,)),
            pltpu.SemaphoreType.DMA,
        ],
        compiler_params=pltpu.CompilerParams(vmem_limit_bytes=36 * 1024 * 1024),
        name="couple",
    )(*operands)


STEPS = 32000.0


def window_kernel(start, green, result, held, sem):
    wide = held.shape[1]
    first = jnp.minimum(start[0] // 128 * 128, green.shape[1] - wide)
    copy = pltpu.make_async_copy(green.at[:, pl.ds(pl.multiple_of(first, 128), wide)], held, sem)
    copy.start()
    copy.wait()
    value = pltpu.roll(held[...], (wide + first - start[0]) % wide, 1)[:, :NOCC]
    top = jnp.max(jnp.abs(value), axis=1, keepdims=True)
    scale_code = jnp.ceil(jnp.log2(jnp.maximum(top, 1e-30)) * 256.0)
    steps = jnp.round(value * (STEPS / jnp.exp2(scale_code * (1.0 / 256.0))))
    result[:, :NOCC] = steps.astype(jnp.int32).astype(jnp.int16)
    result[:, NOCC:] = jnp.broadcast_to(scale_code, (value.shape[0], 128)).astype(jnp.int32).astype(jnp.int16)


def coded_window(green, start):
    rows = green.shape[0]
    return pl.pallas_call(
        window_kernel,
        out_shape=jax.ShapeDtypeStruct((rows, NOCC + 128), jnp.int16),
        in_specs=[pl.BlockSpec(memory_space=pltpu.SMEM), pl.BlockSpec(memory_space=pl.ANY)],
        out_specs=pl.BlockSpec(memory_space=pltpu.VMEM),
        scratch_shapes=[pltpu.VMEM((rows, NOCC + 128), jnp.float32), pltpu.SemaphoreType.DMA],
        name="window",
    )(start, green)


def decoded(code, width):
    number = code.astype(jnp.int32).astype(jnp.float32)
    return number[:, :width] * (jnp.exp2(number[:, width : width + 1] / 256.0) / STEPS)


def upper_blocks(count):
    return [(i, j) for i in range(count) for j in range(i, count)]


def rows_times_rows(left, right):
    return lax.dot_general(left, right, (((1,), (1,)), ((), ())), preferred_element_type=jnp.float32)


def half_of(array, which):
    half = array.shape[0] // 2
    return array[pl.ds(pl.multiple_of(which * half, half), half), :]


def message_rows(array, message, piece):
    start = lax.axis_index("blk") % 2 * (array.shape[0] // 2) + (lax.axis_index("virt") // 2 + message) % 2 * piece
    return array[pl.ds(pl.multiple_of(start, piece), piece), :]


def between_rows(array, piece):
    near = half_of(array, lax.axis_index("blk") % 2)
    return rows_times_rows(near[:piece, :], near[piece:, :])


def across_rows(array, message, piece):
    return rows_times_rows(message_rows(array, message, piece), half_of(array, 1 - lax.axis_index("blk") % 2))


def own_join_kernel(piece, mine, between, *rest):
    acrosses, corners = rest[:2], rest[2:4]
    between[...] = between_rows(mine, piece)
    for message in range(2):
        rows = message_rows(mine, message, piece)
        corners[message][...] = rows_times_rows(rows, rows)
        acrosses[message][...] = across_rows(mine, message, piece)


def first_join_kernel(piece, theirs, between_part, across_part, between, across):
    between[...] = (between_part[...] + between_rows(theirs, piece)).astype(jnp.bfloat16)
    across[...] = (across_part[...] + across_rows(theirs, 0, piece)).astype(jnp.bfloat16)


def second_join_kernel(piece, edge, theirs, across_part, *rest):
    corner_parts, (across, *corners) = rest[:2], rest[2:5]
    for message in range(2):
        rows = message_rows(theirs, message, piece)
        block = corner_parts[message][...] + rows_times_rows(rows, rows)
        for at, (i, j) in enumerate(upper_blocks(piece // edge)):
            corners[message][at * edge : (at + 1) * edge, :] = block[
                i * edge : (i + 1) * edge, j * edge : (j + 1) * edge
            ].astype(jnp.bfloat16)
    across[...] = (across_part[...] + across_rows(theirs, 1, piece)).astype(jnp.bfloat16)


def join(kernel, shapes, operands):
    return pl.pallas_call(
        kernel,
        out_shape=shapes,
        in_specs=[pl.BlockSpec(memory_space=pltpu.VMEM)] * len(operands),
        out_specs=[pl.BlockSpec(memory_space=pltpu.VMEM)] * len(shapes),
        compiler_params=pltpu.CompilerParams(vmem_limit_bytes=28 * 1024 * 1024),
    )(*operands)


def own_join(mine, piece):
    square, wide = (jax.ShapeDtypeStruct((piece, width), jnp.float32) for width in (piece, mine.shape[0] // 2))
    return join(functools.partial(own_join_kernel, piece), [square, wide, wide, square, square], (mine,))


def first_join(theirs, between_part, across_part, piece):
    shapes = [jax.ShapeDtypeStruct((piece, width), jnp.bfloat16) for width in (piece, theirs.shape[0] // 2)]
    operands = (theirs, between_part, across_part)
    return join(functools.partial(first_join_kernel, piece), shapes, operands)


def second_join(theirs, across_part, corner_part, other_corner_part, piece, edge):
    packed = jax.ShapeDtypeStruct((len(upper_blocks(piece // edge)) * edge, edge), jnp.bfloat16)
    shapes = [jax.ShapeDtypeStruct((piece, theirs.shape[0] // 2), jnp.bfloat16), packed, packed]
    operands = (theirs, across_part, corner_part, other_corner_part)
    return join(functools.partial(second_join_kernel, piece, edge), shapes, operands)


def near_kernel(piece, edge, factor, link, passed, corner, other_corner, result, made, *rest):
    held, sems, out_sem = rest[:4], rest[4], rest[5]
    half = 2 * piece
    virt = lax.axis_index("virt")
    operands = (corner, other_corner, link, passed)
    copies = [pltpu.make_async_copy(ref, target, sems.at[at]) for at, (ref, target) in enumerate(zip(operands, held))]
    for copy in copies:
        copy.start()
    corner_h, other_corner_h, link_h, passed_h = held

    def store(start, value):
        made[:, pl.ds(pl.multiple_of(start, edge), piece)] = value * factor

    copies[0].wait()
    copies[1].wait()
    count = piece // edge
    blocks = {}
    for at, place in enumerate(upper_blocks(count)):
        rows = slice(at * edge, (at + 1) * edge)
        blocks[place] = corner_h[rows, :].astype(jnp.float32) + other_corner_h[rows, :].astype(jnp.float32)
    rows = [
        jnp.concatenate([blocks[i, j] if i <= j else blocks[j, i].T for j in range(count)], axis=1)
        for i in range(count)
    ]
    store(virt % 2 * piece, jnp.concatenate(rows, axis=0))
    copies[2].wait()
    copies[3].wait()

    @pl.when(virt % 2 == 0)
    def _():
        store(piece, link_h[...])

    @pl.when(virt % 2 == 1)
    def _():
        store(0, passed_h[...].astype(jnp.float32).T)

    columns = pl.ds(pl.multiple_of(virt // 2 * half, half), half)
    copy = pltpu.make_async_copy(made, result.at[:, columns], out_sem)
    copy.start()
    copy.wait()


def far_kernel(factor, begun, side, other_side, result, made, sem):
    half = made.shape[1]
    made[...] = (side[...].astype(jnp.float32) + other_side[...].astype(jnp.float32)) * factor
    columns = pl.ds(pl.multiple_of((1 - lax.axis_index("virt") // 2) * half, half), half)
    copy = pltpu.make_async_copy(made, result.at[:, columns], sem)
    copy.start()
    copy.wait()


def assemble(link, passed, sides, corners, piece, edge, factor):
    half = 2 * piece
    result = jax.ShapeDtypeStruct((piece, 2 * half), jnp.float32)
    anywhere = pl.BlockSpec(memory_space=pl.ANY)
    begun = pl.pallas_call(
        functools.partial(near_kernel, piece, edge, factor),
        out_shape=result,
        in_specs=[anywhere] * 4,
        out_specs=anywhere,
        scratch_shapes=[pltpu.VMEM((piece, half), jnp.float32)]
        + [pltpu.VMEM(array.shape, array.dtype) for array in (*corners, link, passed)]
        + [pltpu.SemaphoreType.DMA((4,)), pltpu.SemaphoreType.DMA],
        compiler_params=pltpu.CompilerParams(vmem_limit_bytes=20 * 1024 * 1024),
        name="near_half",
    )(link, passed, *corners)
    return pl.pallas_call(
        functools.partial(far_kernel, factor),
        out_shape=result,
        in_specs=[anywhere] + [pl.BlockSpec(memory_space=pltpu.VMEM)] * 2,
        out_specs=anywhere,
        input_output_aliases={0: 0},
        scratch_shapes=[pltpu.VMEM((piece, half), jnp.float32), pltpu.SemaphoreType.DMA],
        compiler_params=pltpu.CompilerParams(vmem_limit_bytes=20 * 1024 * 1024),
        name="far_half",
    )(begun, *sides)


def per_device(integral_tiles, tile_panel, tile_row, tile_col, green_factor, window_start):
    count = lax.axis_size("blk")
    virt_count = lax.axis_size("virt")
    tile_count, edge = integral_tiles.shape[1], integral_tiles.shape[2]
    slots = max(2, 2 * tile_count // count)
    order = offset_order(count)
    middle = STOPS // 2
    everyone = [(block, virt) for block in range(count) for virt in range(virt_count)]

    packed = pack(integral_tiles[0], tile_panel[0, :, 0], tile_row, tile_col, count, slots, order)
    sent = []
    for offset, message in zip(order, packed):
        pairs = [
            (block * virt_count + virt, place_of(partner(block, offset, count), virt, virt_count))
            for block, virt in everyone
        ]
        sent.append(lax.ppermute(message, AXES, pairs))

    window = coded_window(green_factor, window_start)
    own = []
    for at in range(middle):
        pairs = []
        for block, virt in everyone:
            odd = virt % 2
            core = (block - odd) % 2
            panel = (block - odd - core - 2 * at + middle) % count
            pairs.append((block * virt_count + virt, (panel + core) * virt_count + virt))
        own.append(lax.ppermute(window, AXES, pairs))
    swap = [(block, block ^ 1) for block in range(count)]
    other = [lax.ppermute(array, "blk", swap) for array in own]
    coarse, fine = [], []
    for part in own + other:
        part = decoded(part, NOCC)
        top = lax.reduce_precision(part, 8, 7)
        coarse.append(top.astype(jnp.bfloat16))
        fine.append((part - top).astype(jnp.bfloat16))
    total = couple(sent, coarse, fine, count, slots, edge)

    mine = total
    theirs = lax.ppermute(mine, "blk", swap)
    piece = PANEL // virt_count
    between, *parts = own_join(mine, piece)
    between, across = first_join(theirs, between, parts[0], piece)
    other_across, *corners = second_join(theirs, *parts[1:], piece, edge)

    def sent_to(array, message=None, group=None):
        pairs = []
        for block, virt in everyone:
            row = block % 2 * 2 + (0 if message is None else (virt // 2 + message) % 2)
            if group is None or virt // 2 == group:
                pairs.append((block * virt_count + virt, (2 * (block // 2) + virt % 2) * virt_count + row))
        return lax.ppermute(array, AXES, pairs)

    links = [sent_to(between, group=group) for group in range(2)]
    sides = [sent_to(across, 0)]
    for message, corner in enumerate(corners):
        corners[message] = sent_to(corner, message)
    sides.append(sent_to(other_across, 1))
    on = [
        (block * virt_count + virt, block * virt_count + virt + 1)
        for block, virt in everyone
        if virt % 2 == 0
    ]
    link = links[0].astype(jnp.float32) + links[1].astype(jnp.float32)
    passed = lax.ppermute(link.astype(jnp.bfloat16), AXES, on)
    return assemble(link, passed, sides, corners, piece, edge, -1.0 / math.sqrt(virt_count * NOCC))


def solution(mesh):
    return jax.shard_map(
        per_device,
        mesh=mesh,
        in_specs=(
            P("virt", "blk", None, None),
            P("virt", "blk", None),
            P("virt", "blk"),
            P("virt", "blk"),
            P("blk", None),
            P(),
        ),
        out_specs=P(("blk", "virt"), None),
        check_vma=False,
    )
```

```python
import functools
import math

import jax
import jax.numpy as jnp
from jax import lax
from jax.experimental import pallas as pl
from jax.experimental.pallas import tpu as pltpu
from jax.sharding import PartitionSpec as P


NOCC = 1024
STOPS = 8
PANEL = 1536
LABEL_ROWS = 16
AXES = ("blk", "virt")


def offset_order(count):
    def key(offset):
        chip = offset // 2
        return (bin(chip).count("1") or count, offset % 2, chip)

    return sorted(range(count), key=key)


def partner(block, offset, count):
    return block ^ offset if count & (count - 1) == 0 else (block + offset) % count


def place_of(panel, slab, virt_count):
    return (2 * (panel // 2) + slab % 2) * virt_count + 2 * (slab // 2) + panel % 2


def pack_kernel(count, slots, order, panel_s, panel_row, row_row, column_row, tiles, *rest):
    made, rest = rest[:count], rest[count:]
    held, label_rows, label_blocks, slot_tile, used, in_sem, out_sem, label_sem = rest
    tile_count, edge = held.shape[0], held.shape[1]
    parts = in_sem.shape[0]
    per_part = tile_count // parts
    me = lax.axis_index("blk")
    loads = [
        pltpu.make_async_copy(
            tiles.at[pl.ds(part * per_part, per_part)],
            held.at[pl.ds(part * per_part, per_part)],
            in_sem.at[part],
        )
        for part in range(parts)
    ]
    for load in loads:
        load.start()
    for panel in range(count):
        used[panel] = 0

    @pl.loop(0, tile_count)
    def _(at):
        panel = panel_s[at]
        slot = used[panel]
        slot_tile[panel * slots + slot] = at
        used[panel] = slot + 1

    panels = panel_row[...]
    square = (tile_count, tile_count)
    one_hot = (panels == lax.broadcasted_iota(jnp.int32, (max(count, 8), tile_count), 0)).astype(jnp.float32)
    earlier = lax.broadcasted_iota(jnp.int32, square, 0) < lax.broadcasted_iota(jnp.int32, square, 1)
    before = jnp.dot(
        one_hot.astype(jnp.bfloat16),
        earlier.astype(jnp.float32).astype(jnp.bfloat16),
        preferred_element_type=jnp.float32,
    )
    rank = jnp.sum(before * one_hot, axis=0, keepdims=True)
    at_slot = jnp.broadcast_to(rank, square).T == lax.broadcasted_iota(jnp.int32, square, 1).astype(jnp.float32)
    code = row_row[...] * STOPS + column_row[...]
    codes = one_hot * (code.astype(jnp.float32) + 1.0)
    label_rows[...] = (
        jnp.dot(
            codes.astype(jnp.bfloat16),
            at_slot.astype(jnp.float32).astype(jnp.bfloat16),
            preferred_element_type=jnp.float32,
        )
        - 1.0
    )
    label_copies = []
    for at, offset in enumerate(order):
        row = label_rows[pl.ds(partner(me, offset, count), 1), :]
        label_blocks[at] = jnp.broadcast_to(row, (LABEL_ROWS, tile_count)).astype(jnp.bfloat16)
        target = made[at].at[pl.ds(slots * edge, LABEL_ROWS)]
        label_copies.append(pltpu.make_async_copy(label_blocks.at[at], target, label_sem.at[at]))
        label_copies[-1].start()
    for load in loads:
        load.wait()
    for offset, target in zip(order, made):
        panel = partner(me, offset, count)

        @pl.loop(0, used[panel])
        def _(slot):
            pltpu.make_async_copy(
                held.at[slot_tile[panel * slots + slot]],
                target.at[pl.ds(pl.multiple_of(slot * edge, edge), edge)],
                out_sem,
            ).start()

    for copy in label_copies:
        copy.wait()
    pltpu.make_async_copy(tiles, held, out_sem).wait()


def pack(tiles, tile_panel, tile_row, tile_col, count, slots, order):
    tile_count, edge = tiles.shape[0], tiles.shape[1]
    shapes = [jax.ShapeDtypeStruct((slots * edge + LABEL_ROWS, edge), tiles.dtype)] * count
    return pl.pallas_call(
        functools.partial(pack_kernel, count, slots, order),
        out_shape=shapes,
        in_specs=[
            pl.BlockSpec(memory_space=pltpu.SMEM),
            pl.BlockSpec(memory_space=pltpu.VMEM),
            pl.BlockSpec(memory_space=pltpu.VMEM),
            pl.BlockSpec(memory_space=pltpu.VMEM),
            pl.BlockSpec(memory_space=pl.ANY),
        ],
        out_specs=[pl.BlockSpec(memory_space=pl.ANY)] * count,
        scratch_shapes=[
            pltpu.VMEM(tiles.shape, tiles.dtype),
            pltpu.VMEM((max(count, 8), tile_count), jnp.float32),
            pltpu.VMEM((count, LABEL_ROWS, tile_count), jnp.bfloat16),
            pltpu.SMEM((count * slots,), jnp.int32),
            pltpu.SMEM((count,), jnp.int32),
            pltpu.SemaphoreType.DMA((4,)),
            pltpu.SemaphoreType.DMA,
            pltpu.SemaphoreType.DMA((count,)),
        ],
        name="pack",
    )(tile_panel, tile_panel.reshape(1, tile_count), tile_row, tile_col, tiles)


def couple_kernel(count, slots, edge, *rest):
    messages, rest = rest[:count], rest[count:]
    coarse, fine, rest = rest[:STOPS], rest[STOPS : 2 * STOPS], rest[2 * STOPS :]
    result, basis, basis_rest, dense, made, label_rows, labels, basis_sem, out_sem = rest
    core = lax.axis_index("blk") % 2
    loads = []
    for at in range(STOPS // 2):
        for half, stop in ((0, 2 * at + core), (STOPS // 2, 2 * at + 1 - core)):
            rows = pl.ds(pl.multiple_of(stop * edge, edge), edge)
            for ref, target in ((coarse[half + at], basis), (fine[half + at], basis_rest)):
                loads.append(pltpu.make_async_copy(ref, target.at[rows], basis_sem.at[len(loads)]))
    height = slots * edge
    for load in loads:
        load.start()
    for at, message in enumerate(messages):
        row = message[pl.ds(height, LABEL_ROWS), :].astype(jnp.float32)[:1]
        filled = jnp.sum((row >= 0.0).astype(jnp.float32), axis=1, keepdims=True)
        lane = lax.broadcasted_iota(jnp.int32, row.shape, 1)
        label_rows[pl.ds(at, 1), :] = jnp.where(lane == edge - 1, filled, row).astype(jnp.int32)
    copy = pltpu.make_async_copy(label_rows, labels, out_sem)
    copy.start()
    dense[...] = jnp.zeros_like(dense)
    copy.wait()
    together = min(4, slots)
    for at, message in enumerate(messages):

        @pl.loop(0, (labels[at, edge - 1] + together - 1) // together)
        def _(group):
            for inner in range(together):
                slot = group * together + inner
                label = labels[at, slot]

                @pl.when(label >= 0)
                def _():
                    rows = pl.ds(pl.multiple_of(label // STOPS * edge, edge), edge)
                    columns = pl.ds(pl.multiple_of(label % STOPS * edge, edge), edge)
                    tile = message[pl.ds(pl.multiple_of(slot * edge, edge), edge), :]
                    dense[rows, columns] += tile.astype(jnp.float32)

    for load in loads:
        load.wait()
    step = PANEL // 4
    for start in range(0, PANEL, step):
        rows = slice(start, start + step)
        value = dense[rows, :]
        high = value.astype(jnp.bfloat16)
        low = (value - high.astype(jnp.float32)).astype(jnp.bfloat16)
        sums = jnp.dot(high, basis_rest[...], preferred_element_type=jnp.float32)
        sums += jnp.dot(low, basis[...], preferred_element_type=jnp.float32)
        sums += jnp.dot(high, basis[...], preferred_element_type=jnp.float32)
        made[rows, :] = sums.astype(jnp.bfloat16)
        pltpu.make_async_copy(made.at[rows], result.at[rows], out_sem).start()
    pltpu.make_async_copy(made, result, out_sem).wait()


def couple(messages, coarse, fine, count, slots, edge):
    operands = [*messages, *coarse, *fine]
    return pl.pallas_call(
        functools.partial(couple_kernel, count, slots, edge),
        out_shape=jax.ShapeDtypeStruct((PANEL, NOCC), jnp.bfloat16),
        in_specs=[pl.BlockSpec(memory_space=pltpu.VMEM)] * count
        + [pl.BlockSpec(memory_space=pl.ANY)] * (2 * STOPS),
        out_specs=pl.BlockSpec(memory_space=pl.ANY),
        scratch_shapes=[
            pltpu.VMEM((STOPS * edge, NOCC), jnp.bfloat16),
            pltpu.VMEM((STOPS * edge, NOCC), jnp.bfloat16),
            pltpu.VMEM((PANEL, STOPS * edge), jnp.float32),
            pltpu.VMEM((PANEL, NOCC), jnp.bfloat16),
            pltpu.VMEM((count, edge), jnp.int32),
            pltpu.SMEM((count, edge), jnp.int32),
            pltpu.SemaphoreType.DMA((2 * STOPS,)),
            pltpu.SemaphoreType.DMA,
        ],
        compiler_params=pltpu.CompilerParams(vmem_limit_bytes=36 * 1024 * 1024),
        name="couple",
    )(*operands)


STEPS = 32000.0


def window_kernel(start, green, result, held, sem):
    wide = held.shape[1]
    first = jnp.minimum(start[0] // 128 * 128, green.shape[1] - wide)
    copy = pltpu.make_async_copy(green.at[:, pl.ds(pl.multiple_of(first, 128), wide)], held, sem)
    copy.start()
    copy.wait()
    value = pltpu.roll(held[...], (wide + first - start[0]) % wide, 1)[:, :NOCC]
    top = jnp.max(jnp.abs(value), axis=1, keepdims=True)
    scale_code = jnp.ceil(jnp.log2(jnp.maximum(top, 1e-30)) * 256.0)
    steps = jnp.round(value * (STEPS / jnp.exp2(scale_code * (1.0 / 256.0))))
    result[:, :NOCC] = steps.astype(jnp.int32).astype(jnp.int16)
    result[:, NOCC:] = jnp.broadcast_to(scale_code, (value.shape[0], 128)).astype(jnp.int32).astype(jnp.int16)


def coded_window(green, start):
    rows = green.shape[0]
    return pl.pallas_call(
        window_kernel,
        out_shape=jax.ShapeDtypeStruct((rows, NOCC + 128), jnp.int16),
        in_specs=[pl.BlockSpec(memory_space=pltpu.SMEM), pl.BlockSpec(memory_space=pl.ANY)],
        out_specs=pl.BlockSpec(memory_space=pltpu.VMEM),
        scratch_shapes=[pltpu.VMEM((rows, NOCC + 128), jnp.float32), pltpu.SemaphoreType.DMA],
        name="window",
    )(start, green)


def decoded(code, width):
    number = code.astype(jnp.int32).astype(jnp.float32)
    return number[:, :width] * (jnp.exp2(number[:, width : width + 1] / 256.0) / STEPS)


def upper_blocks(count):
    return [(i, j) for i in range(count) for j in range(i, count)]


def rows_times_rows(left, right):
    return lax.dot_general(left, right, (((1,), (1,)), ((), ())), preferred_element_type=jnp.float32)


def half_of(array, which):
    half = array.shape[0] // 2
    return array[pl.ds(pl.multiple_of(which * half, half), half), :]


def message_rows(array, message, piece):
    start = lax.axis_index("blk") % 2 * (array.shape[0] // 2) + (lax.axis_index("virt") // 2 + message) % 2 * piece
    return array[pl.ds(pl.multiple_of(start, piece), piece), :]


def between_rows(array, piece):
    near = half_of(array, lax.axis_index("blk") % 2)
    return rows_times_rows(near[:piece, :], near[piece:, :])


def across_rows(array, message, piece):
    return rows_times_rows(message_rows(array, message, piece), half_of(array, 1 - lax.axis_index("blk") % 2))


def own_join_kernel(piece, mine, between, *rest):
    acrosses, corners = rest[:2], rest[2:4]
    between[...] = between_rows(mine, piece)
    for message in range(2):
        rows = message_rows(mine, message, piece)
        corners[message][...] = rows_times_rows(rows, rows)
        acrosses[message][...] = across_rows(mine, message, piece)


def between_kernel(piece, theirs, between_part, between):
    between[...] = (between_part[...] + between_rows(theirs, piece)).astype(jnp.bfloat16)


def first_join_kernel(piece, theirs, across_part, across):
    across[...] = (across_part[...] + across_rows(theirs, 0, piece)).astype(jnp.bfloat16)


def second_join_kernel(piece, edge, theirs, across_part, *rest):
    corner_parts, (across, *corners) = rest[:2], rest[2:5]
    for message in range(2):
        rows = message_rows(theirs, message, piece)
        block = corner_parts[message][...] + rows_times_rows(rows, rows)
        for at, (i, j) in enumerate(upper_blocks(piece // edge)):
            corners[message][at * edge : (at + 1) * edge, :] = block[
                i * edge : (i + 1) * edge, j * edge : (j + 1) * edge
            ].astype(jnp.bfloat16)
    across[...] = (across_part[...] + across_rows(theirs, 1, piece)).astype(jnp.bfloat16)


def join(kernel, shapes, operands):
    return pl.pallas_call(
        kernel,
        out_shape=shapes,
        in_specs=[pl.BlockSpec(memory_space=pltpu.VMEM)] * len(operands),
        out_specs=[pl.BlockSpec(memory_space=pltpu.VMEM)] * len(shapes),
        compiler_params=pltpu.CompilerParams(vmem_limit_bytes=28 * 1024 * 1024),
    )(*operands)


def own_join(mine, piece):
    square, wide = (jax.ShapeDtypeStruct((piece, width), jnp.float32) for width in (piece, mine.shape[0] // 2))
    return join(functools.partial(own_join_kernel, piece), [square, wide, wide, square, square], (mine,))


def between_join(theirs, between_part, piece):
    shapes = [jax.ShapeDtypeStruct((piece, piece), jnp.bfloat16)]
    return join(functools.partial(between_kernel, piece), shapes, (theirs, between_part))[0]


def first_join(theirs, across_part, piece):
    shapes = [jax.ShapeDtypeStruct((piece, theirs.shape[0] // 2), jnp.bfloat16)]
    return join(functools.partial(first_join_kernel, piece), shapes, (theirs, across_part))[0]


def second_join(theirs, across_part, corner_part, other_corner_part, piece, edge):
    packed = jax.ShapeDtypeStruct((len(upper_blocks(piece // edge)) * edge, edge), jnp.bfloat16)
    shapes = [jax.ShapeDtypeStruct((piece, theirs.shape[0] // 2), jnp.bfloat16), packed, packed]
    operands = (theirs, across_part, corner_part, other_corner_part)
    return join(functools.partial(second_join_kernel, piece, edge), shapes, operands)


def near_kernel(piece, edge, factor, link, passed, corner, other_corner, result, made, *rest):
    held, sems, out_sem = rest[:4], rest[4], rest[5]
    half = 2 * piece
    virt = lax.axis_index("virt")
    operands = (corner, other_corner, link, passed)
    copies = [pltpu.make_async_copy(ref, target, sems.at[at]) for at, (ref, target) in enumerate(zip(operands, held))]
    for copy in copies:
        copy.start()
    corner_h, other_corner_h, link_h, passed_h = held

    def store(start, value):
        made[:, pl.ds(pl.multiple_of(start, edge), piece)] = value * factor

    copies[0].wait()
    copies[1].wait()
    count = piece // edge
    blocks = {}
    for at, place in enumerate(upper_blocks(count)):
        rows = slice(at * edge, (at + 1) * edge)
        blocks[place] = corner_h[rows, :].astype(jnp.float32) + other_corner_h[rows, :].astype(jnp.float32)
    rows = [
        jnp.concatenate([blocks[i, j] if i <= j else blocks[j, i].T for j in range(count)], axis=1)
        for i in range(count)
    ]
    store(virt % 2 * piece, jnp.concatenate(rows, axis=0))
    copies[2].wait()
    copies[3].wait()

    @pl.when(virt % 2 == 0)
    def _():
        store(piece, link_h[...])

    @pl.when(virt % 2 == 1)
    def _():
        store(0, passed_h[...].astype(jnp.float32).T)

    columns = pl.ds(pl.multiple_of(virt // 2 * half, half), half)
    copy = pltpu.make_async_copy(made, result.at[:, columns], out_sem)
    copy.start()
    copy.wait()


def far_kernel(factor, begun, side, other_side, result, made, sem):
    half = made.shape[1]
    made[...] = (side[...].astype(jnp.float32) + other_side[...].astype(jnp.float32)) * factor
    columns = pl.ds(pl.multiple_of((1 - lax.axis_index("virt") // 2) * half, half), half)
    copy = pltpu.make_async_copy(made, result.at[:, columns], sem)
    copy.start()
    copy.wait()


def assemble(link, passed, sides, corners, piece, edge, factor):
    half = 2 * piece
    result = jax.ShapeDtypeStruct((piece, 2 * half), jnp.float32)
    anywhere = pl.BlockSpec(memory_space=pl.ANY)
    begun = pl.pallas_call(
        functools.partial(near_kernel, piece, edge, factor),
        out_shape=result,
        in_specs=[anywhere] * 4,
        out_specs=anywhere,
        scratch_shapes=[pltpu.VMEM((piece, half), jnp.float32)]
        + [pltpu.VMEM(array.shape, array.dtype) for array in (*corners, link, passed)]
        + [pltpu.SemaphoreType.DMA((4,)), pltpu.SemaphoreType.DMA],
        compiler_params=pltpu.CompilerParams(vmem_limit_bytes=20 * 1024 * 1024),
        name="near_half",
    )(link, passed, *corners)
    return pl.pallas_call(
        functools.partial(far_kernel, factor),
        out_shape=result,
        in_specs=[anywhere] + [pl.BlockSpec(memory_space=pltpu.VMEM)] * 2,
        out_specs=anywhere,
        input_output_aliases={0: 0},
        scratch_shapes=[pltpu.VMEM((piece, half), jnp.float32), pltpu.SemaphoreType.DMA],
        compiler_params=pltpu.CompilerParams(vmem_limit_bytes=20 * 1024 * 1024),
        name="far_half",
    )(begun, *sides)


def per_device(integral_tiles, tile_panel, tile_row, tile_col, green_factor, window_start):
    count = lax.axis_size("blk")
    virt_count = lax.axis_size("virt")
    tile_count, edge = integral_tiles.shape[1], integral_tiles.shape[2]
    slots = max(2, 2 * tile_count // count)
    order = offset_order(count)
    middle = STOPS // 2
    everyone = [(block, virt) for block in range(count) for virt in range(virt_count)]

    packed = pack(integral_tiles[0], tile_panel[0, :, 0], tile_row, tile_col, count, slots, order)
    sent = []
    for offset, message in zip(order, packed):
        pairs = [
            (block * virt_count + virt, place_of(partner(block, offset, count), virt, virt_count))
            for block, virt in everyone
        ]
        sent.append(lax.ppermute(message, AXES, pairs))

    window = coded_window(green_factor, window_start)
    own = []
    for at in range(middle):
        pairs = []
        for block, virt in everyone:
            odd = virt % 2
            core = (block - odd) % 2
            panel = (block - odd - core - 2 * at + middle) % count
            pairs.append((block * virt_count + virt, (panel + core) * virt_count + virt))
        own.append(lax.ppermute(window, AXES, pairs))
    swap = [(block, block ^ 1) for block in range(count)]
    other = [lax.ppermute(array, "blk", swap) for array in own]
    coarse, fine = [], []
    for part in own + other:
        part = decoded(part, NOCC)
        top = lax.reduce_precision(part, 8, 7)
        coarse.append(top.astype(jnp.bfloat16))
        fine.append((part - top).astype(jnp.bfloat16))
    total = couple(sent, coarse, fine, count, slots, edge)

    mine = total
    theirs = lax.ppermute(mine, "blk", swap)
    piece = PANEL // virt_count
    between, *parts = own_join(mine, piece)
    between = between_join(theirs, between, piece)
    across = first_join(theirs, parts[0], piece)
    other_across, *corners = second_join(theirs, *parts[1:], piece, edge)

    def sent_to(array, message=None, group=None):
        pairs = []
        for block, virt in everyone:
            row = block % 2 * 2 + (0 if message is None else (virt // 2 + message) % 2)
            if group is None or virt // 2 == group:
                pairs.append((block * virt_count + virt, (2 * (block // 2) + virt % 2) * virt_count + row))
        return lax.ppermute(array, AXES, pairs)

    links = []
    for group in range(2):
        links.append(sent_to(between, group=group))
    sides = [sent_to(across, 0)]
    for message, corner in enumerate(corners):
        corners[message] = sent_to(corner, message)
    sides.append(sent_to(other_across, 1))
    on = [
        (block * virt_count + virt, block * virt_count + virt + 1)
        for block, virt in everyone
        if virt % 2 == 0
    ]
    link = links[0].astype(jnp.float32) + links[1].astype(jnp.float32)
    passed = lax.ppermute(link.astype(jnp.bfloat16), AXES, on)
    return assemble(link, passed, sides, corners, piece, edge, -1.0 / math.sqrt(virt_count * NOCC))


def solution(mesh):
    return jax.shard_map(
        per_device,
        mesh=mesh,
        in_specs=(
            P("virt", "blk", None, None),
            P("virt", "blk", None),
            P("virt", "blk"),
            P("virt", "blk"),
            P("blk", None),
            P(),
        ),
        out_specs=P(("blk", "virt"), None),
        check_vma=False,
    )
```
